256 devices in a mesh: gx: 16 (over y_lo, z), gy: 16 (over y_hi, x, core).
Axes of the slice: x: 4, y: 4 (y_hi: 2, y_lo: 2; y = y_hi * 2 + y_lo), z: 8, core: 2. Of those that a mesh axis runs over, the one named last changes fastest.
Arguments:
- adjoint_in: float32 [57, 4, 128, 2048], P(None, None, 'gx', 'gy'), may hold values from -6 to 6
- populations_early: bfloat16 [57, 4, 128, 2048], P(None, None, 'gx', 'gy'), may hold values from 0.019897461 to 0.099609375
- populations_late: bfloat16 [57, 4, 128, 2048], P(None, None, 'gx', 'gy'), may hold values from 0.019897461 to 0.099609375
- dipoles_early: bfloat16 [3, 4, 128, 2048], P(None, None, 'gx', 'gy'), may hold values from -4 to 4
- dipoles_late: bfloat16 [3, 4, 128, 2048], P(None, None, 'gx', 'gy'), may hold values from -4 to 4
Outputs:
- adjoint_out: float32 [57, 4, 128, 2048], P(None, None, 'gx', 'gy')
The draws below stay inside these ranges and needn't reach their ends.
All inputs are finite; a program needn't handle non-finite values.
Results may differ from the reference program's by a relative error of at most 0.0003.
Values sent between devices are 32-bit elements; how exact they have to be, the bound alone decides.
A program may use at most 128 MiB of HBM per device.

```python
import jax
import jax.numpy as jnp
from jax import lax

POPS = 57
BX = 8
PLANES = 4
NX = 128
NY = 2048


def levels(stream_key, dims, split, smallest, top_value):
    level = 1.0
    for axis_at, parts in split:
        draws = jax.random.uniform(jax.random.fold_in(jax.random.fold_in(stream_key, 6), axis_at), (parts,), jnp.float32, smallest / len(split), top_value / len(split))
        level = level * jnp.repeat(jnp.exp(draws), dims[axis_at] // parts).reshape((-1,) + (1,) * (len(dims) - 1 - axis_at))
    return level


def gaussian(own_key, dims, scale, limit, split=(), held_as=jnp.bfloat16):
    loudness = levels(own_key, dims, split, -0.22, 0.18) if split else 1.0
    values = jax.random.normal(own_key, dims, jnp.float32) * scale * loudness
    return jnp.minimum(jnp.maximum(values, -limit), limit).astype(held_as)


def setup_inputs(seed: int = 0) -> dict:
    key_of = jax.random.split(jax.random.key(seed), 6)
    adjoint_in = gaussian(key_of[0], (POPS, PLANES, NX, NY), 1.0, 6.0, ((2, 16), (3, 16)), jnp.float32)
    populations_early = jnp.clip(0.019897461 + 0.079711914 * jax.random.uniform(key_of[1], (POPS, PLANES, NX, NY), jnp.float32) ** levels(key_of[1], (POPS, PLANES, NX, NY), ((2, 16), (3, 16)), -0.2, 0.2), 0.019897461, 0.099609375).astype(jnp.bfloat16)
    populations_late = jnp.clip(0.019897461 + 0.079711914 * jax.random.uniform(key_of[2], (POPS, PLANES, NX, NY), jnp.float32) ** levels(key_of[2], (POPS, PLANES, NX, NY), ((2, 16), (3, 16)), -0.2, 0.2), 0.019897461, 0.099609375).astype(jnp.bfloat16)
    dipoles_early = gaussian(key_of[3], (3, PLANES, NX, NY), 1.0, 4.0, ((2, 16), (3, 16)))
    dipoles_late = gaussian(key_of[4], (3, PLANES, NX, NY), 1.0, 4.0, ((2, 16), (3, 16)))
    return dict(adjoint_in=adjoint_in, populations_early=populations_early, populations_late=populations_late, dipoles_early=dipoles_early, dipoles_late=dipoles_late)


VELOCITY = ((1, 0, 0), (-1, 0, 0), (0, 1, 0), (0, -1, 0), (1, 1, 0), (-1, -1, 0), (1, -1, 0), (-1, 1, 0), (1, 0, 1), (-1, 0, -1), (1, 0, -1), (-1, 0, 1), (0, 1, 1), (0, -1, -1), (0, 1, -1), (0, -1, 1), (0, 0, 0), (0, 0, 1), (0, 0, -1))
WEIGHT = (1.0 / 18.0,) * 4 + (1.0 / 36.0,) * 12 + (1.0 / 3.0, 1.0 / 18.0, 1.0 / 18.0)
RELAXATION = (1.0, 1.0, 1.25)
COUPLING = ((0.0, 1.2, -0.6), (1.2, 0.0, -0.6), (-0.6, -0.6, -0.3))
DIPOLE_COUPLING = 0.5
CHARGE = (1.0, -1.0)

def neighbour(padded, shift_x, shift_y, shift_z):
    row_count = padded.shape[2] - 2
    col_count = padded.shape[3] - 2
    window = padded[:, :, 1 + shift_x:1 + shift_x + row_count, 1 + shift_y:1 + shift_y + col_count]
    return jnp.roll(window, -shift_z, axis=1)

def stencils(field_pad):
    shape = (field_pad.shape[1], field_pad.shape[2] - 2, field_pad.shape[3] - 2)
    sums = [jnp.zeros(shape, jnp.float32)] * 21
    for q in range(19):
        if q == 16:
            continue
        c = VELOCITY[q]
        weight = WEIGHT[q]
        nearby = neighbour(field_pad, c[0], c[1], c[2])
        projected = c[0] * nearby[3] + c[1] * nearby[4] + c[2] * nearby[5]
        contrast = nearby[0] - nearby[1]
        for d in range(3):
            if c[d] == 0:
                continue
            for s in range(3):
                sums[3 * s + d] = sums[3 * s + d] + weight * c[d] * nearby[s]
            sums[9 + d] = sums[9 + d] + weight * c[d] * projected * nearby[2]
            for j in range(3):
                if c[j] != 0:
                    sums[12 + 3 * d + j] = sums[12 + 3 * d + j] + weight * c[d] * c[j] * contrast
    return jnp.stack(sums)

def forces(potential, dipole, coupled):
    pieces = []
    for s in range(3):
        for d in range(3):
            mixture = COUPLING[s][0] * coupled[d] + COUPLING[s][1] * coupled[3 + d] + COUPLING[s][2] * coupled[6 + d]
            amount = -potential[s] * mixture
            if s < 2:
                amount = amount - 2.0 * DIPOLE_COUPLING * CHARGE[s] * potential[s] * coupled[9 + d]
            else:
                turned = coupled[12 + 3 * d] * dipole[0] + coupled[13 + 3 * d] * dipole[1] + coupled[14 + 3 * d] * dipole[2]
                amount = amount + 2.0 * DIPOLE_COUPLING * potential[2] * turned
            pieces.append(amount)
    return jnp.stack(pieces)

def collide(populations, forcing):
    shaped = populations.reshape((3, 19) + populations.shape[1:])
    density = lax.optimization_barrier(jnp.sum(shaped, axis=1))
    density_sum = lax.optimization_barrier(jnp.sum(density, axis=0))
    flows = lax.optimization_barrier(jnp.sum(shaped, axis=0))
    momentum = []
    for d in range(3):
        amount = jnp.zeros_like(density_sum)
        for q in range(19):
            if VELOCITY[q][d] != 0:
                amount = amount + VELOCITY[q][d] * flows[q]
        momentum.append(amount / density_sum)
    collided = []
    for s in range(3):
        drifts = [momentum[d] + RELAXATION[s] * forcing[3 * s + d] / density[s] for d in range(3)]
        square = drifts[0] * drifts[0] + drifts[1] * drifts[1] + drifts[2] * drifts[2]
        for q in range(19):
            c = VELOCITY[q]
            projected = c[0] * drifts[0] + c[1] * drifts[1] + c[2] * drifts[2]
            equilibrium = WEIGHT[q] * density[s] * (1.0 + 3.0 * projected + 4.5 * projected * projected - 1.5 * square)
            collided.append(shaped[s, q] - (shaped[s, q] - equilibrium) / RELAXATION[s])
    return jnp.stack(collided)

def spread_back(cot_pad, dipole):
    returned = [jnp.zeros(dipole.shape[1:], jnp.float32)] * 3
    for q in range(19):
        if q == 16:
            continue
        c = VELOCITY[q]
        weight = WEIGHT[q]
        nearby = neighbour(cot_pad, -c[0], -c[1], -c[2])
        projected = c[0] * dipole[0] + c[1] * dipole[1] + c[2] * dipole[2]
        tensor = jnp.zeros(dipole.shape[1:], jnp.float32)
        for d in range(3):
            if c[d] == 0:
                continue
            for s in range(3):
                returned[s] = returned[s] + weight * c[d] * nearby[3 * s + d]
            returned[2] = returned[2] + weight * c[d] * projected * nearby[9 + d]
            for j in range(3):
                if c[j] != 0:
                    tensor = tensor + c[d] * c[j] * nearby[12 + 3 * d + j]
        returned[0] = returned[0] + weight * tensor
        returned[1] = returned[1] - weight * tensor
    return jnp.stack(returned)

def saved_field(saved_pops, dipole):
    populations = saved_pops.astype(jnp.float32)
    density = lax.optimization_barrier(jnp.sum(populations.reshape((3, 19) + populations.shape[1:]), axis=1))
    return jnp.concatenate([1.0 - jnp.exp(-density), dipole.astype(jnp.float32)], axis=0)

def pull_all(padded):
    pulled = []
    for s in range(3):
        for q in range(19):
            c = VELOCITY[q]
            pulled.append(neighbour(padded[s * 19 + q:s * 19 + q + 1], c[0], c[1], c[2])[0])
    return jnp.stack(pulled)

def local_adjoint(populations, potential, dipole, coupled, stream):

    def forward(population_arg, potential_arg, coupled_arg):
        return collide(population_arg, forces(potential_arg, dipole, coupled_arg))
    unused, pullback = jax.vjp(forward, populations, potential, coupled)
    return pullback(stream)

def combine(grad_pops, grad_potential, potential):
    grad_density = grad_potential * (1.0 - potential)
    shaped = grad_pops.reshape((3, 19) + grad_pops.shape[1:])
    return (shaped + grad_density[:, None]).reshape(grad_pops.shape)

def wrap_pad(array):
    return jnp.pad(array, ((0, 0), (0, 0), (1, 1), (1, 1)), mode='wrap')

def reverse_ref(adjoint, saved_pops, dipoles):
    stream = pull_all(wrap_pad(adjoint))
    field = saved_field(saved_pops, dipoles)
    coupled = stencils(wrap_pad(field))
    potential = field[:3]
    dipole = field[3:]

    def block_step(block_index, carry):
        offset = (block_index * BX).astype(jnp.int32)

        def slice_block(array):
            return lax.dynamic_slice_in_dim(array, offset, BX, axis=2)
        pieces = local_adjoint(slice_block(saved_pops).astype(jnp.float32), slice_block(potential), slice_block(dipole), slice_block(coupled), slice_block(stream))
        return tuple((lax.dynamic_update_slice_in_dim(whole_array, piece_array, offset, axis=2) for whole_array, piece_array in zip(carry, pieces)))
    initial = (jnp.zeros(stream.shape, jnp.float32), jnp.zeros(potential.shape, jnp.float32), jnp.zeros(coupled.shape, jnp.float32))
    grad_pops, grad_potential, grad_coupled = lax.fori_loop(0, NX // BX, block_step, initial)
    total_potential = grad_potential + spread_back(wrap_pad(grad_coupled), dipole)
    return combine(grad_pops, total_potential, potential)

def reference(adjoint_in, populations_early, populations_late, dipoles_early, dipoles_late):
    adjoint_mid = reverse_ref(adjoint_in, populations_late, dipoles_late)
    return reverse_ref(adjoint_mid, populations_early, dipoles_early)
```

```python
import jax
import jax.numpy as jnp
from jax import lax
from jax.experimental import pallas as pl
from jax.experimental.pallas import tpu as pltpu
from jax.sharding import PartitionSpec as P

MESH = pl.DeviceIdType.MESH
VELOCITY = (
    (1, 0, 0),
    (-1, 0, 0),
    (0, 1, 0),
    (0, -1, 0),
    (1, 1, 0),
    (-1, -1, 0),
    (1, -1, 0),
    (-1, 1, 0),
    (1, 0, 1),
    (-1, 0, -1),
    (1, 0, -1),
    (-1, 0, 1),
    (0, 1, 1),
    (0, -1, -1),
    (0, 1, -1),
    (0, -1, 1),
    (0, 0, 0),
    (0, 0, 1),
    (0, 0, -1),
)
TAU = (1.0, 1.0, 1.25)
G = ((0.0, 1.2, -0.6), (1.2, 0.0, -0.6), (-0.6, -0.6, -0.3))
ORDER = (1, 5, 7, 9, 11, 2, 3, 12, 13, 14, 15, 16, 17, 18, 0, 4, 6, 8, 10)
SLOT = {q: i for i, q in enumerate(ORDER)}
F32 = jnp.float32


def up_y(v):
    return pltpu.roll(v, 127, 1)


def dn_y(v):
    return pltpu.roll(v, 1, 1)


def shift_y(v, cy):
    return v if cy == 0 else (up_y(v) if cy == 1 else dn_y(v))


def near(ld, f):
    n = dict(
        c=ld(f, 0, 0),
        xp=ld(f, 1, 0),
        xm=ld(f, -1, 0),
        zp=ld(f, 0, 1),
        zm=ld(f, 0, -1),
        pp=ld(f, 1, 1),
        pm=ld(f, 1, -1),
        mp=ld(f, -1, 1),
        mm=ld(f, -1, -1),
    )
    n["dx"] = n["xp"] - n["xm"]
    n["dz"] = n["zp"] - n["zm"]
    n["sx"] = n["xp"] + n["xm"]
    n["sz"] = n["zp"] + n["zm"]
    return n


def corner(n):
    return (n["pp"] + n["mm"]) + (n["pm"] + n["mp"])


def cross(n):
    return (n["pp"] + n["mm"]) - (n["pm"] + n["mp"])


def corner_x(n):
    return (n["pp"] - n["mm"]) + (n["pm"] - n["mp"])


def corner_z(n):
    return (n["pp"] - n["mm"]) - (n["pm"] - n["mp"])


def gradient(n):
    h = 2.0 * n["c"] + n["sx"] + n["sz"]
    r = dict(
        hp=up_y(h),
        hm=dn_y(h),
        dxp=up_y(n["dx"]),
        dxm=dn_y(n["dx"]),
        dzp=up_y(n["dz"]),
        dzm=dn_y(n["dz"]),
    )
    gx = 2.0 * n["dx"] + corner_x(n) + (r["dxp"] + r["dxm"])
    gz = 2.0 * n["dz"] + corner_z(n) + (r["dzp"] + r["dzm"])
    return (gx, r["hp"] - r["hm"], gz), r


def second(sx, sz, cor, crs, r):
    xx = 2.0 * sx + cor + (up_y(sx) + dn_y(sx))
    zz = 2.0 * sz + cor + (up_y(sz) + dn_y(sz))
    return dict(
        xx=xx,
        yy=r["hp"] + r["hm"],
        zz=zz,
        xy=r["dxp"] - r["dxm"],
        yz=r["dzp"] - r["dzm"],
        xz=crs,
    )


def vector_stencil(nx, ny, nz):
    px = 2.0 * nx["sx"] + corner(nx) + cross(nz)
    px = px + up_y(nx["sx"] + ny["dx"]) + dn_y(nx["sx"] - ny["dx"])
    pz = 2.0 * nz["sz"] + corner(nz) + cross(nx)
    pz = pz + up_y(nz["sz"] + ny["dz"]) + dn_y(nz["sz"] - ny["dz"])
    a = 2.0 * ny["c"] + ny["sx"] + ny["sz"]
    b = nx["dx"] + nz["dz"]
    return px, up_y(a + b) + dn_y(a - b), pz


def divergence(nx, ny, nz):
    u = nx["dx"] + nz["dz"]
    v = 2.0 * ny["c"] + ny["sx"] + ny["sz"]
    return 2.0 * u + corner_x(nx) + corner_z(nz) + up_y(u + v) + dn_y(u - v)


def moments_of(g):
    p = {}
    m = {}
    for q in (0, 2, 4, 6, 8, 10, 12, 14, 17):
        p[q] = g[q] + g[q + 1]
        m[q] = g[q] - g[q + 1]
    xy, xz, yz = p[4] + p[6], p[8] + p[10], p[12] + p[14]
    ax, ay, az = 2.0 * p[0], 2.0 * p[2], 2.0 * p[17]
    a = 12.0 * g[16] + (ax + ay + az) + (xy + xz + yz)
    b = (
        2.0 * m[0] + (m[4] + m[6]) + (m[8] + m[10]),
        2.0 * m[2] + (m[4] - m[6]) + (m[12] + m[14]),
        2.0 * m[17] + (m[8] - m[10]) + (m[12] - m[14]),
    )
    c = dict(
        xx=ax + xy + xz,
        yy=ay + xy + yz,
        zz=az + xz + yz,
        xy=p[4] - p[6],
        xz=p[8] - p[10],
        yz=p[12] - p[14],
    )
    return a, b, c


def pick_potentials(rho, d):
    psi = [1.0 - jnp.exp(-r) for r in rho]
    mixed = [
        1.2 * psi[1] - 0.6 * psi[2],
        1.2 * psi[0] - 0.6 * psi[2],
        -0.6 * (psi[0] + psi[1]) - 0.3 * psi[2],
    ]
    return psi, mixed + [d[j] * psi[2] for j in range(3)]


def thrusts(ld, d):
    grads, rolled, sums = [], [], []
    for s in range(3):
        n = near(ld, s)
        g, r = gradient(n)
        grads.append(g)
        if s < 2:
            rolled.append(r)
            sums.append((n["sx"], n["sz"], corner(n), cross(n)))
    diff = [b - a for a, b in zip(*sums)]
    r = {key: rolled[1][key] - rolled[0][key] for key in rolled[0]}
    m = second(*diff, r)
    e = [near(ld, 3 + j) for j in range(3)]
    p = vector_stencil(*e)
    k = 1.0 / 36.0
    k2 = 1.0 / (36.0 * 1.2)
    turned = (
        m["xx"] * d[0] + m["xy"] * d[1] + m["xz"] * d[2],
        m["xy"] * d[0] + m["yy"] * d[1] + m["yz"] * d[2],
        m["xz"] * d[0] + m["yz"] * d[1] + m["zz"] * d[2],
    )
    t0 = [-k * (grads[0][i] + p[i]) for i in range(3)]
    t1 = [k * (p[i] - grads[1][i]) for i in range(3)]
    t2 = [k2 * turned[i] - k * grads[2][i] for i in range(3)]
    return t0 + t1 + t2


def local_adjoint(mom, rho, u, psi, t, d):
    x, e_val, wt, ratio = [], [], [], []
    m = [None] * 3
    for s in range(3):
        a, b, c = mom[s]
        ratio.append(TAU[s] * psi[s] / rho[s])
        ts = t[3 * s : 3 * s + 3]
        v = [u[i] + ratio[s] * ts[i] for i in range(3)]
        cv = (
            c["xx"] * v[0] + c["xy"] * v[1] + c["xz"] * v[2],
            c["xy"] * v[0] + c["yy"] * v[1] + c["yz"] * v[2],
            c["xz"] * v[0] + c["yz"] * v[1] + c["zz"] * v[2],
        )
        k = 1.0 / (36.0 * TAU[s])
        b3 = [3.0 * b[i] for i in range(3)]
        a3 = 3.0 * a
        w = [b3[i] + 9.0 * cv[i] - a3 * v[i] for i in range(3)]
        half = (b3[0] + w[0]) * v[0] + (b3[1] + w[1]) * v[1] + (b3[2] + w[2]) * v[2]
        e_val.append(k * a + (0.5 * k) * half)
        w = [k * w[i] for i in range(3)]
        wt.append(w[0] * ts[0] + w[1] * ts[1] + w[2] * ts[2])
        for i in range(3):
            term = rho[s] * w[i]
            m[i] = term if s == 0 else m[i] + term
        tp = TAU[s] * psi[s]
        x.extend(tp * w[i] for i in range(3))
    inverse = 1.0 / (rho[0] + rho[1] + rho[2])
    m = [m[i] * inverse for i in range(3)]
    mu = m[0] * u[0] + m[1] * u[1] + m[2] * u[2]
    dens = [e_val[s] + wt[s] * (TAU[s] * (1.0 - psi[s]) - ratio[s]) - mu for s in range(3)]
    y = x[6:9]
    kxx, kyy, kzz = y[0] * d[0], y[1] * d[1], y[2] * d[2]
    kept = [
        kxx,
        kyy,
        kzz,
        y[0] * d[1] + y[1] * d[0],
        y[0] * d[2] + y[2] * d[0],
        y[1] * d[2] + y[2] * d[1],
        kxx + kyy,
        kyy + kzz,
        kxx + kzz,
    ]
    return x + kept, m, dens


def spread(ld, dens, psi, d):
    n = [[near(ld, 3 * s + i) for i in range(3)] for s in range(3)]
    y = [divergence(*n[s]) for s in range(3)]
    diff = [{key: n[0][i][key] - n[1][i][key] for key in n[0][i]} for i in range(3)]
    z = vector_stencil(*diff)
    xx, zz, a3, kxz = near(ld, 9), near(ld, 11), near(ld, 17), near(ld, 13)
    a1, a2, kxy, kyz = near(ld, 15), near(ld, 16), near(ld, 12), near(ld, 14)
    u = 2.0 * ld(10, 0, 0) + a1["sx"] + a2["sz"]
    v = kxy["dx"] + kyz["dz"]
    quad = 2.0 * (xx["sx"] + zz["sz"]) + corner(a3) + cross(kxz) + up_y(u + v) + dn_y(u - v)
    k = 1.0 / 36.0
    back = [
        1.2 * y[1] - 0.6 * y[2] + quad,
        1.2 * y[0] - 0.6 * y[2] - quad,
        -0.6 * (y[0] + y[1]) - 0.3 * y[2] - (d[0] * z[0] + d[1] * z[1] + d[2] * z[2]),
    ]
    return [dens[s] + (k * (1.0 - psi[s])) * back[s] for s in range(3)]


def late_moments(ld, pulled):
    x, y, z = (near(ld, i) for i in range(3))
    axx, azz = 2.0 * x["dx"], 2.0 * z["dz"]
    ayy = 2.0 * (up_y(y["c"]) - dn_y(y["c"]))
    exz = corner_x(x) + corner_z(z)
    exy = up_y(x["dx"] + y["sx"]) + dn_y(x["dx"] - y["sx"])
    eyz = up_y(z["dz"] + y["sz"]) + dn_y(z["dz"] - y["sz"])
    a_m = (axx + ayy + azz) + (exy + exz + eyz)
    b_m = vector_stencil(x, y, z)
    c_m = dict(
        xx=axx + exy + exz,
        yy=ayy + exy + eyz,
        zz=azz + exz + eyz,
        xy=up_y(y["dx"] + x["sx"]) + dn_y(y["dx"] - x["sx"]),
        yz=up_y(y["dz"] + z["sz"]) + dn_y(y["dz"] - z["sz"]),
        xz=corner_z(x) + corner_x(z),
    )
    extra = moments_of(pulled)
    out = []
    for s in range(3):
        n = near(ld, 3 + s)
        g, r = gradient(n)
        c = second(n["sx"], n["sz"], corner(n), cross(n), r)
        a = 12.0 * n["c"] + 2.0 * (n["sx"] + n["sz"]) + corner(n) + c["yy"] + a_m
        b = [g[i] + b_m[i] for i in range(3)]
        c = {key: c[key] + c_m[key] for key in c}
        if s == 2:
            a = a + 0.2 * extra[0]
            b = [b[i] + 0.2 * extra[1][i] for i in range(3)]
            c = {key: c[key] + 0.2 * extra[2][key] for key in c}
        out.append((a, b, c))
    return out


def kernel(
    size_x,
    size_y,
    a_in,
    pe_in,
    pl_in,
    de_in,
    dl_in,
    o_out,
    A,
    NE,
    NL,
    DE,
    DL,
    OUT,
    F,
    FL,
    FE,
    FM,
    FG,
    PO,
    PLX,
    PRX,
    PGO,
    PGL,
    PGR,
    PMO,
    PML,
    PMR,
    SA,
    SG,
    SL,
    SE,
    QM,
    QS,
    TB,
    SI,
    XM,
    XS,
    LM,
    LS,
    MS,
    TS,
    lsem,
    ssem,
    rsem,
):
    gx, gy = lax.axis_index("gx"), lax.axis_index("gy")
    xu, xd = lax.rem(gx + 1, size_x), lax.rem(gx + size_x - 1, size_x)
    yr, yl = lax.rem(gy + 1, size_y), lax.rem(gy + size_y - 1, size_y)
    everyone = [(xu, gy), (xd, gy), (gx, yr), (gx, yl), (xu, yr), (xu, yl), (xd, yr), (xd, yl)]
    barrier = pltpu.get_barrier_semaphore()
    for who in everyone:
        pl.semaphore_signal(barrier, inc=1, device_id=who, device_id_type=MESH)
    loads = [
        pltpu.make_async_copy(src, dst, lsem.at[i])
        for i, (src, dst) in enumerate(
            ((pl_in, NL), (dl_in, DL), (a_in, A), (pe_in, NE), (de_in, DE))
        )
    ]
    for copy in loads:
        copy.start()

    lane = lax.broadcasted_iota(jnp.int32, (8, 128), 1)
    sub = lax.broadcasted_iota(jnp.int32, (8, 128), 0)
    c16 = lane % 16
    group16 = lane // 16
    group4 = lane // 4

    count = [0]

    def remote(src, dst, who):
        i = count[0]
        count[0] += 1
        return pltpu.make_async_remote_copy(
            src_ref=src,
            dst_ref=dst,
            send_sem=ssem.at[i],
            recv_sem=rsem.at[i],
            device_id=who,
            device_id_type=MESH,
        )

    def row_copies(ref, lead, base, depth, up, down):
        out = []
        for z in range(4):
            row = base + 12 * z
            if up:
                out.append(
                    remote(
                        ref.at[lead + (pl.ds(row + 10 - depth, depth),)],
                        ref.at[lead + (pl.ds(row + 2 - depth, depth),)],
                        (xu, gy),
                    )
                )
            if down:
                out.append(
                    remote(
                        ref.at[lead + (pl.ds(row + 2, depth),)],
                        ref.at[lead + (pl.ds(row + 10, depth),)],
                        (xd, gy),
                    )
                )
        return out

    def pop_rows(ref, lead, base):
        return (
            row_copies(ref, lead + (pl.ds(0, 5),), base, 2, True, False)
            + row_copies(ref, lead + (pl.ds(14, 5),), base, 2, False, True)
            + row_copies(ref, lead + (pl.ds(5, 9),), base, 1, True, True)
        )

    def edge_copies(own, left, right, tiles):
        out = []
        for who, ref, src, dst in (
            ((xu, yr), left, (6, 2), 2),
            ((xd, yr), left, (0, 2), 12),
            ((xu, yl), right, (6, 2), 2),
            ((xd, yl), right, (0, 2), 12),
            ((gx, yr), left, (0, 8), 4),
            ((gx, yl), right, (0, 8), 4),
        ):
            out.append(
                remote(
                    own.at[tiles, pl.ds(*src)],
                    ref.at[tiles, pl.ds(dst, src[1])],
                    who,
                )
            )
        return out

    def pack(acc, v, z, slot):
        moved = pltpu.roll(v, (32 * z + 4 * slot + 2) % 128, 1)
        return moved if acc is None else jnp.where(group4 == 8 * z + slot, moved, acc)

    def strip_of(own, cy, left, right, slot):
        acc = None
        for z in range(4):
            for h in range(2):
                v = own(z, h)
                base = 32 * z + 16 * h
                w = jnp.where(
                    c16 < 8,
                    pltpu.roll(v, (base - 122 - cy) % 128, 1),
                    pltpu.roll(v, (base + 10 - cy) % 128, 1),
                )
                acc = w if acc is None else jnp.where(group16 == 2 * z + h, w, acc)
        odd = group16 % 2 == 1
        if cy >= 0 or True:
            r = [pltpu.roll(right(h), (16 * h + 4 - cy - 4 * slot) % 128, 1) for h in range(2)]
            r = jnp.where(odd, r[1], r[0])
            acc = jnp.where((c16 >= 6 - cy) & (c16 < 8), r, acc)
        l = [pltpu.roll(left(h), (16 * h + 8 - cy - 4 * slot) % 128, 1) for h in range(2)]
        l = jnp.where(odd, l[1], l[0])
        return jnp.where((c16 >= 8) & (c16 <= 9 - cy), l, acc)

    def store_strip(ref, f, v):
        ref[f, 1, 8:16, :] = v
        ref[f, 0, 8:16, :] = pltpu.roll(v, 32, 1)
        ref[f, 2, 8:16, :] = pltpu.roll(v, 96, 1)

    def strip_loader(ref):
        return lambda f, dx, dz: ref[f, 1 + dz, 8 + dx : 16 + dx, :]

    def flat_loader(ref, k):
        return lambda f, dx, dz: ref[f, pl.ds(8 * k + (16 + dx + 12 * dz), 8), :]

    def over_tiles(body):
        lax.fori_loop(0, 6, lambda k, carry: (body(k), carry)[1], 0)

    def saved(pops, dips, ref, tile0):
        acc = [None, None]
        for z in range(4):
            flow = [None] * 19
            dens = []
            for s in range(3):
                total = None
                for q in range(19):
                    f = pops[19 * s + q, z].astype(F32)
                    total = f if total is None else total + f
                    flow[q] = f if s == 0 else flow[q] + f
                dens.append(total)
            inverse = 1.0 / (dens[0] + dens[1] + dens[2])
            fields = list(dens)
            for i in range(3):
                amount = None
                for q in range(19):
                    c = VELOCITY[q][i]
                    if c != 0:
                        term = flow[q] if c > 0 else -flow[q]
                        amount = term if amount is None else amount + term
                fields.append(amount * inverse)
            fields.extend(dips[i, z].astype(F32) for i in range(3))
            for f in range(9):
                ref[f, 12 * z + 2 : 12 * z + 10, :] = fields[f]
                acc[f // 8] = pack(acc[f // 8], fields[f], z, f % 8)
        PO[tile0] = acc[0]
        PO[tile0 + 1] = acc[1]

    loads[0].wait()
    loads[1].wait()
    saved(NL, DL, FL, 9)

    loads[2].wait()

    def spread_pops(s, carry):
        acc = [None] * 3
        for o, q in enumerate(ORDER):
            for z in range(4):
                v = A[19 * s + q, (z + VELOCITY[q][2]) % 4]
                F[s, o, 8 + 12 * z + 2 : 8 + 12 * z + 10, :] = v
                acc[o // 8] = pack(acc[o // 8], v, z, o % 8)
        for i in range(3):
            PO[3 * s + i] = acc[i]
        return carry

    lax.fori_loop(0, 3, spread_pops, 0)

    pl.semaphore_wait(barrier, 8)
    every = (pl.ds(0, 9),)
    first = edge_copies(PO, PLX, PRX, pl.ds(0, 11))
    first += row_copies(FL, every, 0, 2, True, True)
    first += pop_rows(F, (pl.ds(0, 3),), 8)
    for copy in first:
        copy.start()

    loads[3].wait()
    loads[4].wait()
    saved(NE, DE, FE, 11)
    second_set = edge_copies(PO, PLX, PRX, pl.ds(11, 2)) + row_copies(FE, every, 0, 2, True, True)
    for copy in second_set:
        copy.start()

    def potentials(ref, strips):
        def body(k):
            rows = pl.ds(8 * k, 8)
            psi, fields = pick_potentials(
                [ref[s, rows, :] for s in range(3)], [ref[6 + i, rows, :] for i in range(3)]
            )
            for s in range(3):
                SI[s, k] = psi[s]
            for f in range(6):
                QM[f, pl.ds(16 + 8 * k, 8), :] = fields[f]
                QM[f, pl.ds(lax.rem(8 * k + 64, 96), 8), :] = fields[f]

        over_tiles(body)
        psi, fields = pick_potentials(
            [strips[s] for s in range(3)], [strips[6 + i] for i in range(3)]
        )
        for s in range(3):
            SI[s, 6] = psi[s]
        for f in range(6):
            store_strip(QS, f, fields[f])

    def all_thrusts(ref, strips):
        def body(k):
            rows = pl.ds(8 * k, 8)
            t = thrusts(flat_loader(QM, k), [ref[6 + i, rows, :] for i in range(3)])
            for f in range(9):
                TB[f, k] = t[f]

        over_tiles(body)
        t = thrusts(strip_loader(QS), [strips[6 + i] for i in range(3)])
        for f in range(9):
            TB[f, 6] = t[f]

    def field_strips(ref, strips, tile0):
        for f in range(9):
            tile, slot = tile0 + f // 8, f % 8
            strips[f] = strip_of(
                lambda z, h: ref[f, 12 * z + 4 * h : 12 * z + 4 * h + 8, :],
                0,
                lambda h: PLX[tile, 2 + 4 * h : 10 + 4 * h, :],
                lambda h: PRX[tile, 2 + 4 * h : 10 + 4 * h, :],
                slot,
            )

    def adjoint_stage(ref, strips, main_moments, strip_moments):
        def one(mom, k, rho, u, d, put_x, put_l):
            psi = [SI[s, k] for s in range(3)]
            t = [TB[f, k] for f in range(9)]
            fields, m, dens = local_adjoint(mom, rho, u, psi, t, d)
            for f in range(18):
                put_x(f, fields[f])
            for i in range(3):
                put_l(i, m[i])
                put_l(3 + i, dens[i])

        def body(k):
            rows = pl.ds(8 * k, 8)

            def put_x(f, v):
                XM[f, pl.ds(16 + 8 * k, 8), :] = v
                XM[f, pl.ds(lax.rem(8 * k + 64, 96), 8), :] = v

            def put_l(f, v):
                LM[f, rows, :] = v

            get = [ref[f, rows, :] for f in range(9)]
            one(main_moments(k), k, get[0:3], get[3:6], get[6:9], put_x, put_l)

        over_tiles(body)

        def put_x(f, v):
            store_strip(XS, f, v)

        def put_l(f, v):
            LS[f, 8:16, :] = v

        get = [strips[f] for f in range(9)]
        one(strip_moments(), 6, get[0:3], get[3:6], get[6:9], put_x, put_l)

    def spread_stage(ref, strips):
        def body(k):
            rows = pl.ds(8 * k, 8)
            new = spread(
                flat_loader(XM, k),
                [LM[3 + s, rows, :] for s in range(3)],
                [SI[s, k] for s in range(3)],
                [ref[6 + i, rows, :] for i in range(3)],
            )
            for s in range(3):
                LM[3 + s, rows, :] = new[s]

        over_tiles(body)
        new = spread(
            strip_loader(XS),
            [LS[3 + s, 8:16, :] for s in range(3)],
            [SI[s, 6] for s in range(3)],
            [strips[6 + i] for i in range(3)],
        )
        for s in range(3):
            LS[3 + s, 8:16, :] = new[s]

    def folded(ref, f):
        low = ref[f, 10:18, :]
        high = pltpu.roll(ref[f, 6:14, :], 112, 1)
        return jnp.where(sub < 4, low, high)

    def with_edges(v, edge, z):
        right = pltpu.roll(edge, (122 - 32 * z) % 128, 1)
        left = pltpu.roll(edge, (-32 * z - 10) % 128, 1)
        return jnp.where(lane >= 126, right, jnp.where(lane < 2, left, v))

    for copy in first:
        copy.wait_recv()

    acc = [None] * 3
    for o, q in enumerate(ORDER):
        cx, cy, cz = VELOCITY[q]
        tile, slot = 6 + o // 8, o % 8
        for z in range(4):
            v = shift_y(F[2, o, 8 + 12 * z + 2 + cx : 8 + 12 * z + 10 + cx, :], cy)
            if cy == -1:
                halo = pltpu.roll(
                    PLX[tile, 4 + cx : 12 + cx, :], (-(32 * z + 4 * slot + 1)) % 128, 1
                )
                v = jnp.where(lane == 0, halo, v)
            if cy == 1:
                halo = pltpu.roll(
                    PRX[tile, 4 + cx : 12 + cx, :], (127 - (32 * z + 4 * slot + 2)) % 128, 1
                )
                v = jnp.where(lane == 127, halo, v)
            to = (z - cz) % 4
            FG[o, 8 + 12 * to + 2 : 8 + 12 * to + 10, :] = v
            acc[o // 8] = pack(acc[o // 8], v, to, slot)
    for i in range(3):
        PGO[i] = acc[i]
    kept = edge_copies(PGO, PGL, PGR, pl.ds(0, 3)) + pop_rows(FG, (), 8)
    for copy in kept:
        copy.start()

    field_strips(FL, SL, 9)
    potentials(FL, SL)
    all_thrusts(FL, SL)

    def pop_strips(s, carry):
        for o, q in enumerate(ORDER):
            cx, cy, _ = VELOCITY[q]
            SA[19 * s + o] = strip_of(
                lambda z, h: F[
                    s, o, 8 + 12 * z + 4 * h + cx : 8 + 12 * z + 4 * h + cx + 8, :
                ],
                cy,
                lambda h: PLX[3 * s + o // 8, 2 + 4 * h + cx : 10 + 4 * h + cx, :],
                lambda h: PRX[3 * s + o // 8, 2 + 4 * h + cx : 10 + 4 * h + cx, :],
                o % 8,
            )
        return carry

    lax.fori_loop(0, 3, pop_strips, 0)

    def pulled_moments(k):
        out = []
        for s in range(3):
            g = {}
            for o, q in enumerate(ORDER):
                cx, cy, _ = VELOCITY[q]
                g[q] = shift_y(F[s, o, pl.ds(8 * k + (8 + cx), 8), :], cy)
            out.append(moments_of(g))
        return out

    def pulled_strip_moments():
        return [moments_of({q: SA[19 * s + SLOT[q]] for q in range(19)}) for s in range(3)]

    adjoint_stage(FL, SL, pulled_moments, pulled_strip_moments)
    spread_stage(FL, SL)

    acc = None
    for f in range(6):
        edge = folded(LS, f)
        for z in range(4):
            v = with_edges(LM[f, 12 * z + 2 : 12 * z + 10, :], edge, z)
            FM[f, 16 + 12 * z + 2 : 16 + 12 * z + 10, :] = v
            acc = pack(acc, v, z, f)
    PMO[0] = acc
    middle = edge_copies(PMO, PML, PMR, pl.ds(0, 1)) + row_copies(
        FM, (pl.ds(0, 6),), 16, 2, True, True
    )
    for copy in middle:
        copy.start()

    for copy in second_set:
        copy.wait_recv()
    field_strips(FE, SE, 11)
    potentials(FE, SE)
    all_thrusts(FE, SE)

    for copy in kept:
        copy.wait_recv()
    for o, q in enumerate(ORDER):
        cx, cy, _ = VELOCITY[q]
        SG[o] = strip_of(
            lambda z, h: FG[o, 8 + 12 * z + 4 * h + cx : 8 + 12 * z + 4 * h + cx + 8, :],
            cy,
            lambda h: PGL[o // 8, 2 + 4 * h + cx : 10 + 4 * h + cx, :],
            lambda h: PGR[o // 8, 2 + 4 * h + cx : 10 + 4 * h + cx, :],
            o % 8,
        )

    for copy in middle:
        copy.wait_recv()
    for f in range(6):
        FM[f, 0:16, :] = FM[f, 48:64, :]
        FM[f, 64:80, :] = FM[f, 16:32, :]
        store_strip(
            MS,
            f,
            strip_of(
                lambda z, h: FM[f, 16 + 12 * z + 4 * h : 16 + 12 * z + 4 * h + 8, :],
                0,
                lambda h: PML[0, 2 + 4 * h : 10 + 4 * h, :],
                lambda h: PMR[0, 2 + 4 * h : 10 + 4 * h, :],
                f,
            ),
        )

    def middle_moments(k):
        g = {}
        for o, q in enumerate(ORDER):
            cx, cy, _ = VELOCITY[q]
            g[q] = shift_y(FG[o, pl.ds(8 * k + (8 + cx), 8), :], cy)
        return late_moments(flat_loader(FM, k), g)

    def middle_strip_moments():
        return late_moments(strip_loader(MS), {q: SG[SLOT[q]] for q in range(19)})

    adjoint_stage(FE, SE, middle_moments, middle_strip_moments)
    spread_stage(FE, SE)

    def along(q, m):
        out = None
        for i in range(3):
            c = VELOCITY[q][i]
            if c != 0:
                term = m[i] if c > 0 else -m[i]
                out = term if out is None else out + term
        return out

    def plus(base, term):
        return base if term is None else base + term

    strip = strip_loader(MS)
    for o, q in enumerate(ORDER):
        cx, cy, cz = VELOCITY[q]
        if cy != 0:
            v = plus(strip(5, cx, cz), along(q, [strip(i, cx, cz) for i in range(3)]))
            TS[o, 8:16, :] = shift_y(v, cy) + 0.2 * SG[o]

    edges = [folded(LS, f) for f in range(6)]
    for z in range(4):
        fin = [with_edges(LM[f, 12 * z + 2 : 12 * z + 10, :], edges[f], z) for f in range(6)]
        for q in range(19):
            cx, cy, cz = VELOCITY[q]
            term = along(q, fin[0:3])
            OUT[q, z] = plus(fin[3], term)
            OUT[19 + q, z] = plus(fin[4], term)
            o = SLOT[q]
            row = 12 * z + 2 + cx
            mid = [FM[i, 16 + row + 12 * cz : 24 + row + 12 * cz, :] for i in (0, 1, 2, 5)]
            v = plus(mid[3], along(q, mid[0:3])) + 0.2 * FG[o, 8 + row : 16 + row, :]
            v = shift_y(v, cy)
            if cy != 0:
                v = with_edges(v, folded(TS, o), z)
            OUT[38 + q, z] = plus(fin[5], term) + 0.2 * v

    done = pltpu.make_async_copy(OUT, o_out, lsem.at[5])
    done.start()
    for copy in first + second_set + kept + middle:
        copy.wait_send()
    done.wait()


N_REMOTE = 6 + 8 + 16 + 6 + 8 + 6 + 16 + 6 + 8


def block(size_x, size_y, *args):
    def vmem(*shape, dtype=F32):
        return pltpu.VMEM(shape, dtype)

    bf = jnp.bfloat16
    scratch = [
        vmem(57, 4, 8, 128),
        vmem(57, 4, 8, 128, dtype=bf),
        vmem(57, 4, 8, 128, dtype=bf),
        vmem(3, 4, 8, 128, dtype=bf),
        vmem(3, 4, 8, 128, dtype=bf),
        vmem(57, 4, 8, 128),
        vmem(3, 19, 64, 128),
        vmem(9, 48, 128),
        vmem(9, 48, 128),
        vmem(6, 80, 128),
        vmem(19, 64, 128),
        vmem(13, 8, 128),
        vmem(13, 16, 128),
        vmem(13, 16, 128),
        vmem(3, 8, 128),
        vmem(3, 16, 128),
        vmem(3, 16, 128),
        vmem(1, 8, 128),
        vmem(1, 16, 128),
        vmem(1, 16, 128),
        vmem(57, 8, 128),
        vmem(19, 8, 128),
        vmem(9, 8, 128),
        vmem(9, 8, 128),
        vmem(6, 96, 128),
        vmem(6, 3, 24, 128),
        vmem(9, 7, 8, 128),
        vmem(3, 7, 8, 128),
        vmem(18, 96, 128),
        vmem(18, 3, 24, 128),
        vmem(6, 48, 128),
        vmem(6, 24, 128),
        vmem(6, 3, 24, 128),
        vmem(19, 24, 128),
        pltpu.SemaphoreType.DMA((6,)),
        pltpu.SemaphoreType.DMA((N_REMOTE,)),
        pltpu.SemaphoreType.DMA((N_REMOTE,)),
    ]
    return pl.pallas_call(
        lambda *refs: kernel(size_x, size_y, *refs),
        out_shape=jax.ShapeDtypeStruct((57, 4, 8, 128), F32),
        in_specs=[pl.BlockSpec(memory_space=pl.ANY)] * 5,
        out_specs=pl.BlockSpec(memory_space=pl.ANY),
        scratch_shapes=scratch,
        compiler_params=pltpu.CompilerParams(collective_id=0, has_side_effects=True),
        name="lattice_adjoint",
    )(*args)


def solution(mesh):
    size_x, size_y = mesh.shape["gx"], mesh.shape["gy"]
    spec = P(None, None, "gx", "gy")
    return jax.shard_map(
        lambda *args: block(size_x, size_y, *args),
        mesh=mesh,
        in_specs=(spec,) * 5,
        out_specs=spec,
        check_vma=False,
    )
```

```python
import jax
import jax.numpy as jnp
from jax import lax
from jax.experimental import pallas as pl
from jax.experimental.pallas import tpu as pltpu
from jax.sharding import PartitionSpec as P

MESH = pl.DeviceIdType.MESH
VELOCITY = (
    (1, 0, 0),
    (-1, 0, 0),
    (0, 1, 0),
    (0, -1, 0),
    (1, 1, 0),
    (-1, -1, 0),
    (1, -1, 0),
    (-1, 1, 0),
    (1, 0, 1),
    (-1, 0, -1),
    (1, 0, -1),
    (-1, 0, 1),
    (0, 1, 1),
    (0, -1, -1),
    (0, 1, -1),
    (0, -1, 1),
    (0, 0, 0),
    (0, 0, 1),
    (0, 0, -1),
)
TAU = (1.0, 1.0, 1.25)
G = ((0.0, 1.2, -0.6), (1.2, 0.0, -0.6), (-0.6, -0.6, -0.3))
ORDER = (1, 5, 7, 9, 11, 2, 3, 12, 13, 14, 15, 16, 17, 18, 0, 4, 6, 8, 10)
SLOT = {q: i for i, q in enumerate(ORDER)}
F32 = jnp.float32


def up_y(v):
    return pltpu.roll(v, 127, 1)


def dn_y(v):
    return pltpu.roll(v, 1, 1)


def shift_y(v, cy):
    return v if cy == 0 else (up_y(v) if cy == 1 else dn_y(v))


def near(ld, f):
    n = dict(
        c=ld(f, 0, 0),
        xp=ld(f, 1, 0),
        xm=ld(f, -1, 0),
        zp=ld(f, 0, 1),
        zm=ld(f, 0, -1),
        pp=ld(f, 1, 1),
        pm=ld(f, 1, -1),
        mp=ld(f, -1, 1),
        mm=ld(f, -1, -1),
    )
    n["dx"] = n["xp"] - n["xm"]
    n["dz"] = n["zp"] - n["zm"]
    n["sx"] = n["xp"] + n["xm"]
    n["sz"] = n["zp"] + n["zm"]
    return n


def corner(n):
    return (n["pp"] + n["mm"]) + (n["pm"] + n["mp"])


def cross(n):
    return (n["pp"] + n["mm"]) - (n["pm"] + n["mp"])


def corner_x(n):
    return (n["pp"] - n["mm"]) + (n["pm"] - n["mp"])


def corner_z(n):
    return (n["pp"] - n["mm"]) - (n["pm"] - n["mp"])


def gradient(n):
    h = 2.0 * n["c"] + n["sx"] + n["sz"]
    r = dict(
        hp=up_y(h),
        hm=dn_y(h),
        dxp=up_y(n["dx"]),
        dxm=dn_y(n["dx"]),
        dzp=up_y(n["dz"]),
        dzm=dn_y(n["dz"]),
    )
    gx = 2.0 * n["dx"] + corner_x(n) + (r["dxp"] + r["dxm"])
    gz = 2.0 * n["dz"] + corner_z(n) + (r["dzp"] + r["dzm"])
    return (gx, r["hp"] - r["hm"], gz), r


def second(sx, sz, cor, crs, r):
    xx = 2.0 * sx + cor + (up_y(sx) + dn_y(sx))
    zz = 2.0 * sz + cor + (up_y(sz) + dn_y(sz))
    return dict(
        xx=xx,
        yy=r["hp"] + r["hm"],
        zz=zz,
        xy=r["dxp"] - r["dxm"],
        yz=r["dzp"] - r["dzm"],
        xz=crs,
    )


def vector_stencil(nx, ny, nz):
    px = 2.0 * nx["sx"] + corner(nx) + cross(nz)
    px = px + up_y(nx["sx"] + ny["dx"]) + dn_y(nx["sx"] - ny["dx"])
    pz = 2.0 * nz["sz"] + corner(nz) + cross(nx)
    pz = pz + up_y(nz["sz"] + ny["dz"]) + dn_y(nz["sz"] - ny["dz"])
    a = 2.0 * ny["c"] + ny["sx"] + ny["sz"]
    b = nx["dx"] + nz["dz"]
    return px, up_y(a + b) + dn_y(a - b), pz


def divergence(nx, ny, nz):
    u = nx["dx"] + nz["dz"]
    v = 2.0 * ny["c"] + ny["sx"] + ny["sz"]
    return 2.0 * u + corner_x(nx) + corner_z(nz) + up_y(u + v) + dn_y(u - v)


def moments_of(g):
    p = {}
    m = {}
    for q in (0, 2, 4, 6, 8, 10, 12, 14, 17):
        p[q] = g[q] + g[q + 1]
        m[q] = g[q] - g[q + 1]
    xy, xz, yz = p[4] + p[6], p[8] + p[10], p[12] + p[14]
    ax, ay, az = 2.0 * p[0], 2.0 * p[2], 2.0 * p[17]
    a = 12.0 * g[16] + (ax + ay + az) + (xy + xz + yz)
    b = (
        2.0 * m[0] + (m[4] + m[6]) + (m[8] + m[10]),
        2.0 * m[2] + (m[4] - m[6]) + (m[12] + m[14]),
        2.0 * m[17] + (m[8] - m[10]) + (m[12] - m[14]),
    )
    c = dict(
        xx=ax + xy + xz,
        yy=ay + xy + yz,
        zz=az + xz + yz,
        xy=p[4] - p[6],
        xz=p[8] - p[10],
        yz=p[12] - p[14],
    )
    return a, b, c


def pick_potentials(rho, d):
    psi = [1.0 - jnp.exp(-r) for r in rho]
    mixed = [
        1.2 * psi[1] - 0.6 * psi[2],
        1.2 * psi[0] - 0.6 * psi[2],
        -0.6 * (psi[0] + psi[1]) - 0.3 * psi[2],
    ]
    return psi, mixed + [d[j] * psi[2] for j in range(3)]


def thrusts(ld, d):
    grads, rolled, sums = [], [], []
    for s in range(3):
        n = near(ld, s)
        g, r = gradient(n)
        grads.append(g)
        if s < 2:
            rolled.append(r)
            sums.append((n["sx"], n["sz"], corner(n), cross(n)))
    diff = [b - a for a, b in zip(*sums)]
    r = {key: rolled[1][key] - rolled[0][key] for key in rolled[0]}
    m = second(*diff, r)
    e = [near(ld, 3 + j) for j in range(3)]
    p = vector_stencil(*e)
    k = 1.0 / 36.0
    k2 = 1.0 / (36.0 * 1.2)
    turned = (
        m["xx"] * d[0] + m["xy"] * d[1] + m["xz"] * d[2],
        m["xy"] * d[0] + m["yy"] * d[1] + m["yz"] * d[2],
        m["xz"] * d[0] + m["yz"] * d[1] + m["zz"] * d[2],
    )
    t0 = [-k * (grads[0][i] + p[i]) for i in range(3)]
    t1 = [k * (p[i] - grads[1][i]) for i in range(3)]
    t2 = [k2 * turned[i] - k * grads[2][i] for i in range(3)]
    return t0 + t1 + t2


def local_adjoint(mom, rho, u, psi, t, d):
    x, e_val, wt, ratio = [], [], [], []
    m = [None] * 3
    for s in range(3):
        a, b, c = mom[s]
        ratio.append(TAU[s] * psi[s] / rho[s])
        ts = t[3 * s : 3 * s + 3]
        v = [u[i] + ratio[s] * ts[i] for i in range(3)]
        cv = (
            c["xx"] * v[0] + c["xy"] * v[1] + c["xz"] * v[2],
            c["xy"] * v[0] + c["yy"] * v[1] + c["yz"] * v[2],
            c["xz"] * v[0] + c["yz"] * v[1] + c["zz"] * v[2],
        )
        k = 1.0 / (36.0 * TAU[s])
        b3 = [3.0 * b[i] for i in range(3)]
        a3 = 3.0 * a
        w = [b3[i] + 9.0 * cv[i] - a3 * v[i] for i in range(3)]
        half = (b3[0] + w[0]) * v[0] + (b3[1] + w[1]) * v[1] + (b3[2] + w[2]) * v[2]
        e_val.append(k * a + (0.5 * k) * half)
        w = [k * w[i] for i in range(3)]
        wt.append(w[0] * ts[0] + w[1] * ts[1] + w[2] * ts[2])
        for i in range(3):
            term = rho[s] * w[i]
            m[i] = term if s == 0 else m[i] + term
        tp = TAU[s] * psi[s]
        x.extend(tp * w[i] for i in range(3))
    inverse = 1.0 / (rho[0] + rho[1] + rho[2])
    m = [m[i] * inverse for i in range(3)]
    mu = m[0] * u[0] + m[1] * u[1] + m[2] * u[2]
    dens = [e_val[s] + wt[s] * (TAU[s] * (1.0 - psi[s]) - ratio[s]) - mu for s in range(3)]
    y = x[6:9]
    kxx, kyy, kzz = y[0] * d[0], y[1] * d[1], y[2] * d[2]
    kept = [
        kxx,
        kyy,
        kzz,
        y[0] * d[1] + y[1] * d[0],
        y[0] * d[2] + y[2] * d[0],
        y[1] * d[2] + y[2] * d[1],
        kxx + kyy,
        kyy + kzz,
        kxx + kzz,
    ]
    return x + kept, m, dens


def spread(ld, dens, psi, d):
    n = [[near(ld, 3 * s + i) for i in range(3)] for s in range(3)]
    y = [divergence(*n[s]) for s in range(3)]
    diff = [{key: n[0][i][key] - n[1][i][key] for key in n[0][i]} for i in range(3)]
    z = vector_stencil(*diff)
    xx, zz, a3, kxz = near(ld, 9), near(ld, 11), near(ld, 17), near(ld, 13)
    a1, a2, kxy, kyz = near(ld, 15), near(ld, 16), near(ld, 12), near(ld, 14)
    u = 2.0 * ld(10, 0, 0) + a1["sx"] + a2["sz"]
    v = kxy["dx"] + kyz["dz"]
    quad = 2.0 * (xx["sx"] + zz["sz"]) + corner(a3) + cross(kxz) + up_y(u + v) + dn_y(u - v)
    k = 1.0 / 36.0
    back = [
        1.2 * y[1] - 0.6 * y[2] + quad,
        1.2 * y[0] - 0.6 * y[2] - quad,
        -0.6 * (y[0] + y[1]) - 0.3 * y[2] - (d[0] * z[0] + d[1] * z[1] + d[2] * z[2]),
    ]
    return [dens[s] + (k * (1.0 - psi[s])) * back[s] for s in range(3)]


def late_moments(ld, pulled):
    x, y, z = (near(ld, i) for i in range(3))
    axx, azz = 2.0 * x["dx"], 2.0 * z["dz"]
    ayy = 2.0 * (up_y(y["c"]) - dn_y(y["c"]))
    exz = corner_x(x) + corner_z(z)
    exy = up_y(x["dx"] + y["sx"]) + dn_y(x["dx"] - y["sx"])
    eyz = up_y(z["dz"] + y["sz"]) + dn_y(z["dz"] - y["sz"])
    a_m = (axx + ayy + azz) + (exy + exz + eyz)
    b_m = vector_stencil(x, y, z)
    c_m = dict(
        xx=axx + exy + exz,
        yy=ayy + exy + eyz,
        zz=azz + exz + eyz,
        xy=up_y(y["dx"] + x["sx"]) + dn_y(y["dx"] - x["sx"]),
        yz=up_y(y["dz"] + z["sz"]) + dn_y(y["dz"] - z["sz"]),
        xz=corner_z(x) + corner_x(z),
    )
    extra = moments_of(pulled)
    out = []
    for s in range(3):
        n = near(ld, 3 + s)
        g, r = gradient(n)
        c = second(n["sx"], n["sz"], corner(n), cross(n), r)
        a = 12.0 * n["c"] + 2.0 * (n["sx"] + n["sz"]) + corner(n) + c["yy"] + a_m
        b = [g[i] + b_m[i] for i in range(3)]
        c = {key: c[key] + c_m[key] for key in c}
        if s == 2:
            a = a + 0.2 * extra[0]
            b = [b[i] + 0.2 * extra[1][i] for i in range(3)]
            c = {key: c[key] + 0.2 * extra[2][key] for key in c}
        out.append((a, b, c))
    return out


def along(q, m):
    out = None
    for i in range(3):
        c = VELOCITY[q][i]
        if c != 0:
            term = m[i] if c > 0 else -m[i]
            out = term if out is None else out + term
    return out

def plus(base, term):
    return base if term is None else base + term


def kernel(
    size_x,
    size_y,
    a_in,
    pe_in,
    pl_in,
    de_in,
    dl_in,
    FIN,
    A,
    NE,
    NL,
    DE,
    DL,
    F,
    FL,
    FE,
    FM,
    FG,
    PO,
    PLX,
    PRX,
    PGO,
    PGL,
    PGR,
    PMO,
    PML,
    PMR,
    SA,
    SG,
    SL,
    SE,
    QM,
    QS,
    TB,
    SI,
    XM,
    XS,
    LM,
    LS,
    MS,
    TS,
    lsem,
    ssem,
    rsem,
):
    gx, gy = lax.axis_index("gx"), lax.axis_index("gy")
    xu, xd = lax.rem(gx + 1, size_x), lax.rem(gx + size_x - 1, size_x)
    yr, yl = lax.rem(gy + 1, size_y), lax.rem(gy + size_y - 1, size_y)
    everyone = [(xu, gy), (xd, gy), (gx, yr), (gx, yl), (xu, yr), (xu, yl), (xd, yr), (xd, yl)]
    barrier = pltpu.get_barrier_semaphore()
    for who in everyone:
        pl.semaphore_signal(barrier, inc=1, device_id=who, device_id_type=MESH)
    loads = [
        pltpu.make_async_copy(src, dst, lsem.at[i])
        for i, (src, dst) in enumerate(
            ((pl_in, NL), (dl_in, DL), (a_in, A), (pe_in, NE), (de_in, DE))
        )
    ]
    for copy in loads:
        copy.start()

    lane = lax.broadcasted_iota(jnp.int32, (8, 128), 1)
    sub = lax.broadcasted_iota(jnp.int32, (8, 128), 0)
    c16 = lane % 16
    group16 = lane // 16
    group4 = lane // 4

    count = [0]

    def remote(src, dst, who):
        i = count[0]
        count[0] += 1
        return pltpu.make_async_remote_copy(
            src_ref=src,
            dst_ref=dst,
            send_sem=ssem.at[i],
            recv_sem=rsem.at[i],
            device_id=who,
            device_id_type=MESH,
        )

    def row_copies(ref, lead, base, depth, up, down):
        out = []
        for z in range(4):
            row = base + 12 * z
            if up:
                out.append(
                    remote(
                        ref.at[lead + (pl.ds(row + 10 - depth, depth),)],
                        ref.at[lead + (pl.ds(row + 2 - depth, depth),)],
                        (xu, gy),
                    )
                )
            if down:
                out.append(
                    remote(
                        ref.at[lead + (pl.ds(row + 2, depth),)],
                        ref.at[lead + (pl.ds(row + 10, depth),)],
                        (xd, gy),
                    )
                )
        return out

    def pop_rows(ref, lead, base):
        return (
            row_copies(ref, lead + (pl.ds(0, 5),), base, 2, True, False)
            + row_copies(ref, lead + (pl.ds(14, 5),), base, 2, False, True)
            + row_copies(ref, lead + (pl.ds(5, 9),), base, 1, True, True)
        )

    def edge_copies(own, left, right, tiles):
        out = []
        for who, ref, src, dst in (
            ((xu, yr), left, (6, 2), 2),
            ((xd, yr), left, (0, 2), 12),
            ((xu, yl), right, (6, 2), 2),
            ((xd, yl), right, (0, 2), 12),
            ((gx, yr), left, (0, 8), 4),
            ((gx, yl), right, (0, 8), 4),
        ):
            out.append(
                remote(
                    own.at[tiles, pl.ds(*src)],
                    ref.at[tiles, pl.ds(dst, src[1])],
                    who,
                )
            )
        return out

    def pack(acc, v, z, slot):
        moved = pltpu.roll(v, (32 * z + 4 * slot + 2) % 128, 1)
        return moved if acc is None else jnp.where(group4 == 8 * z + slot, moved, acc)

    def strip_of(own, cy, left, right, slot):
        acc = None
        for z in range(4):
            for h in range(2):
                v = own(z, h)
                base = 32 * z + 16 * h
                w = jnp.where(
                    c16 < 8,
                    pltpu.roll(v, (base - 122 - cy) % 128, 1),
                    pltpu.roll(v, (base + 10 - cy) % 128, 1),
                )
                acc = w if acc is None else jnp.where(group16 == 2 * z + h, w, acc)
        odd = group16 % 2 == 1
        if cy >= 0 or True:
            r = [pltpu.roll(right(h), (16 * h + 4 - cy - 4 * slot) % 128, 1) for h in range(2)]
            r = jnp.where(odd, r[1], r[0])
            acc = jnp.where((c16 >= 6 - cy) & (c16 < 8), r, acc)
        l = [pltpu.roll(left(h), (16 * h + 8 - cy - 4 * slot) % 128, 1) for h in range(2)]
        l = jnp.where(odd, l[1], l[0])
        return jnp.where((c16 >= 8) & (c16 <= 9 - cy), l, acc)

    def store_strip(ref, f, v):
        ref[f, 1, 8:16, :] = v
        ref[f, 0, 8:16, :] = pltpu.roll(v, 32, 1)
        ref[f, 2, 8:16, :] = pltpu.roll(v, 96, 1)

    def strip_loader(ref):
        return lambda f, dx, dz: ref[f, 1 + dz, 8 + dx : 16 + dx, :]

    def flat_loader(ref, k):
        return lambda f, dx, dz: ref[f, pl.ds(8 * k + (16 + dx + 12 * dz), 8), :]

    def over_tiles(body):
        lax.fori_loop(0, 6, lambda k, carry: (body(k), carry)[1], 0, unroll=3)

    def saved(pops, dips, ref, tile0):
        acc = [None, None]
        for z in range(4):
            flow = [None] * 19
            dens = []
            for s in range(3):
                total = None
                for q in range(19):
                    f = pops[19 * s + q, z].astype(F32)
                    total = f if total is None else total + f
                    flow[q] = f if s == 0 else flow[q] + f
                dens.append(total)
            inverse = 1.0 / (dens[0] + dens[1] + dens[2])
            fields = list(dens)
            for i in range(3):
                amount = None
                for q in range(19):
                    c = VELOCITY[q][i]
                    if c != 0:
                        term = flow[q] if c > 0 else -flow[q]
                        amount = term if amount is None else amount + term
                fields.append(amount * inverse)
            fields.extend(dips[i, z].astype(F32) for i in range(3))
            for f in range(9):
                ref[f, 12 * z + 2 : 12 * z + 10, :] = fields[f]
                acc[f // 8] = pack(acc[f // 8], fields[f], z, f % 8)
        PO[tile0] = acc[0]
        PO[tile0 + 1] = acc[1]

    loads[0].wait()
    loads[1].wait()
    saved(NL, DL, FL, 9)

    loads[2].wait()

    def spread_pops(s, carry):
        acc = [None] * 3
        for o, q in enumerate(ORDER):
            for z in range(4):
                v = A[19 * s + q, (z + VELOCITY[q][2]) % 4]
                F[s, o, 8 + 12 * z + 2 : 8 + 12 * z + 10, :] = v
                acc[o // 8] = pack(acc[o // 8], v, z, o % 8)
        for i in range(3):
            PO[3 * s + i] = acc[i]
        return carry

    lax.fori_loop(0, 3, spread_pops, 0)

    pl.semaphore_wait(barrier, 8)
    every = (pl.ds(0, 9),)
    first = edge_copies(PO, PLX, PRX, pl.ds(0, 11))
    first += row_copies(FL, every, 0, 2, True, True)
    rows = pop_rows(F, (pl.ds(0, 3),), 8)
    for copy in first + rows:
        copy.start()

    loads[3].wait()
    loads[4].wait()
    saved(NE, DE, FE, 11)
    second_set = edge_copies(PO, PLX, PRX, pl.ds(11, 2)) + row_copies(FE, every, 0, 2, True, True)
    for copy in second_set:
        copy.start()

    def potentials(ref, strips):
        def body(k):
            rows = pl.ds(8 * k, 8)
            psi, fields = pick_potentials(
                [ref[s, rows, :] for s in range(3)], [ref[6 + i, rows, :] for i in range(3)]
            )
            for s in range(3):
                SI[s, k] = psi[s]
            for f in range(6):
                QM[f, pl.ds(16 + 8 * k, 8), :] = fields[f]
                QM[f, pl.ds(lax.rem(8 * k + 64, 96), 8), :] = fields[f]

        over_tiles(body)
        psi, fields = pick_potentials(
            [strips[s] for s in range(3)], [strips[6 + i] for i in range(3)]
        )
        for s in range(3):
            SI[s, 6] = psi[s]
        for f in range(6):
            store_strip(QS, f, fields[f])

    def all_thrusts(ref, strips):
        def body(k):
            rows = pl.ds(8 * k, 8)
            t = thrusts(flat_loader(QM, k), [ref[6 + i, rows, :] for i in range(3)])
            for f in range(9):
                TB[f, k] = t[f]

        over_tiles(body)
        t = thrusts(strip_loader(QS), [strips[6 + i] for i in range(3)])
        for f in range(9):
            TB[f, 6] = t[f]

    def field_strips(ref, strips, tile0):
        for f in range(9):
            tile, slot = tile0 + f // 8, f % 8
            strips[f] = strip_of(
                lambda z, h: ref[f, 12 * z + 4 * h : 12 * z + 4 * h + 8, :],
                0,
                lambda h: PLX[tile, 2 + 4 * h : 10 + 4 * h, :],
                lambda h: PRX[tile, 2 + 4 * h : 10 + 4 * h, :],
                slot,
            )

    def adjoint_stage(ref, strips, main_moments, strip_moments):
        def one(mom, k, rho, u, d, put_x, put_l):
            psi = [SI[s, k] for s in range(3)]
            t = [TB[f, k] for f in range(9)]
            fields, m, dens = local_adjoint(mom, rho, u, psi, t, d)
            for f in range(18):
                put_x(f, fields[f])
            for i in range(3):
                put_l(i, m[i])
                put_l(3 + i, dens[i])

        def body(k):
            rows = pl.ds(8 * k, 8)

            def put_x(f, v):
                XM[f, pl.ds(16 + 8 * k, 8), :] = v
                XM[f, pl.ds(lax.rem(8 * k + 64, 96), 8), :] = v

            def put_l(f, v):
                LM[f, rows, :] = v

            get = [ref[f, rows, :] for f in range(9)]
            one(main_moments(k), k, get[0:3], get[3:6], get[6:9], put_x, put_l)

        over_tiles(body)

        def put_x(f, v):
            store_strip(XS, f, v)

        def put_l(f, v):
            LS[f, 8:16, :] = v

        get = [strips[f] for f in range(9)]
        one(strip_moments(), 6, get[0:3], get[3:6], get[6:9], put_x, put_l)

    def spread_stage(ref, strips):
        def body(k):
            rows = pl.ds(8 * k, 8)
            new = spread(
                flat_loader(XM, k),
                [LM[3 + s, rows, :] for s in range(3)],
                [SI[s, k] for s in range(3)],
                [ref[6 + i, rows, :] for i in range(3)],
            )
            for s in range(3):
                LM[3 + s, rows, :] = new[s]

        over_tiles(body)
        new = spread(
            strip_loader(XS),
            [LS[3 + s, 8:16, :] for s in range(3)],
            [SI[s, 6] for s in range(3)],
            [strips[6 + i] for i in range(3)],
        )
        for s in range(3):
            LS[3 + s, 8:16, :] = new[s]

    def folded(ref, f):
        low = ref[f, 10:18, :]
        high = pltpu.roll(ref[f, 6:14, :], 112, 1)
        return jnp.where(sub < 4, low, high)

    def with_edges(v, edge, z):
        right = pltpu.roll(edge, (122 - 32 * z) % 128, 1)
        left = pltpu.roll(edge, (-32 * z - 10) % 128, 1)
        return jnp.where(lane >= 126, right, jnp.where(lane < 2, left, v))

    for copy in first:
        copy.wait_recv()
    field_strips(FL, SL, 9)
    potentials(FL, SL)
    all_thrusts(FL, SL)
    for copy in rows:
        copy.wait_recv()

    acc = [None] * 3
    for o, q in enumerate(ORDER):
        cx, cy, cz = VELOCITY[q]
        tile, slot = 6 + o // 8, o % 8
        for z in range(4):
            v = shift_y(F[2, o, 8 + 12 * z + 2 + cx : 8 + 12 * z + 10 + cx, :], cy)
            if cy == -1:
                halo = pltpu.roll(
                    PLX[tile, 4 + cx : 12 + cx, :], (-(32 * z + 4 * slot + 1)) % 128, 1
                )
                v = jnp.where(lane == 0, halo, v)
            if cy == 1:
                halo = pltpu.roll(
                    PRX[tile, 4 + cx : 12 + cx, :], (127 - (32 * z + 4 * slot + 2)) % 128, 1
                )
                v = jnp.where(lane == 127, halo, v)
            to = (z - cz) % 4
            FG[o, 8 + 12 * to + 2 : 8 + 12 * to + 10, :] = v
            acc[o // 8] = pack(acc[o // 8], v, to, slot)
    for i in range(3):
        PGO[i] = acc[i]
    kept = edge_copies(PGO, PGL, PGR, pl.ds(0, 3)) + pop_rows(FG, (), 8)
    for copy in kept:
        copy.start()

    def pop_strips(s, carry):
        for o, q in enumerate(ORDER):
            cx, cy, _ = VELOCITY[q]
            SA[19 * s + o] = strip_of(
                lambda z, h: F[
                    s, o, 8 + 12 * z + 4 * h + cx : 8 + 12 * z + 4 * h + cx + 8, :
                ],
                cy,
                lambda h: PLX[3 * s + o // 8, 2 + 4 * h + cx : 10 + 4 * h + cx, :],
                lambda h: PRX[3 * s + o // 8, 2 + 4 * h + cx : 10 + 4 * h + cx, :],
                o % 8,
            )
        return carry

    lax.fori_loop(0, 3, pop_strips, 0)

    def pulled_moments(k):
        out = []
        for s in range(3):
            g = {}
            for o, q in enumerate(ORDER):
                cx, cy, _ = VELOCITY[q]
                g[q] = shift_y(F[s, o, pl.ds(8 * k + (8 + cx), 8), :], cy)
            out.append(moments_of(g))
        return out

    def pulled_strip_moments():
        return [moments_of({q: SA[19 * s + SLOT[q]] for q in range(19)}) for s in range(3)]

    adjoint_stage(FL, SL, pulled_moments, pulled_strip_moments)
    spread_stage(FL, SL)

    acc = None
    for f in range(6):
        edge = folded(LS, f)
        for z in range(4):
            v = with_edges(LM[f, 12 * z + 2 : 12 * z + 10, :], edge, z)
            FM[f, 16 + 12 * z + 2 : 16 + 12 * z + 10, :] = v
            acc = pack(acc, v, z, f)
    PMO[0] = acc
    middle = edge_copies(PMO, PML, PMR, pl.ds(0, 1)) + row_copies(
        FM, (pl.ds(0, 6),), 16, 2, True, True
    )
    for copy in middle:
        copy.start()

    for copy in second_set:
        copy.wait_recv()
    field_strips(FE, SE, 11)
    potentials(FE, SE)
    all_thrusts(FE, SE)

    for copy in kept:
        copy.wait_recv()
    for o, q in enumerate(ORDER):
        cx, cy, _ = VELOCITY[q]
        SG[o] = strip_of(
            lambda z, h: FG[o, 8 + 12 * z + 4 * h + cx : 8 + 12 * z + 4 * h + cx + 8, :],
            cy,
            lambda h: PGL[o // 8, 2 + 4 * h + cx : 10 + 4 * h + cx, :],
            lambda h: PGR[o // 8, 2 + 4 * h + cx : 10 + 4 * h + cx, :],
            o % 8,
        )

    for copy in middle:
        copy.wait_recv()
    for f in range(6):
        FM[f, 0:16, :] = FM[f, 48:64, :]
        FM[f, 64:80, :] = FM[f, 16:32, :]
        store_strip(
            MS,
            f,
            strip_of(
                lambda z, h: FM[f, 16 + 12 * z + 4 * h : 16 + 12 * z + 4 * h + 8, :],
                0,
                lambda h: PML[0, 2 + 4 * h : 10 + 4 * h, :],
                lambda h: PMR[0, 2 + 4 * h : 10 + 4 * h, :],
                f,
            ),
        )

    def middle_moments(k):
        g = {}
        for o, q in enumerate(ORDER):
            cx, cy, _ = VELOCITY[q]
            g[q] = shift_y(FG[o, pl.ds(8 * k + (8 + cx), 8), :], cy)
        return late_moments(flat_loader(FM, k), g)

    def middle_strip_moments():
        return late_moments(strip_loader(MS), {q: SG[SLOT[q]] for q in range(19)})

    adjoint_stage(FE, SE, middle_moments, middle_strip_moments)
    spread_stage(FE, SE)

    strip = strip_loader(MS)
    for o, q in enumerate(ORDER):
        cx, cy, cz = VELOCITY[q]
        if cy != 0:
            v = plus(strip(5, cx, cz), along(q, [strip(i, cx, cz) for i in range(3)]))
            TS[o, 8:16, :] = shift_y(v, cy) + 0.2 * SG[o]

    edges = [folded(LS, f) for f in range(6)]
    for z in range(4):
        for f in range(6):
            FIN[f, z] = with_edges(LM[f, 12 * z + 2 : 12 * z + 10, :], edges[f], z)
        for o, q in enumerate(ORDER):
            cx, cy, cz = VELOCITY[q]
            row = 12 * z + 2 + cx
            mid = [FM[i, 16 + row + 12 * cz : 24 + row + 12 * cz, :] for i in (0, 1, 2, 5)]
            v = plus(mid[3], along(q, mid[0:3])) + 0.2 * FG[o, 8 + row : 16 + row, :]
            v = shift_y(v, cy)
            if cy != 0:
                v = with_edges(v, folded(TS, o), z)
            FIN[6 + q, z] = 0.2 * v

    for copy in first + rows + second_set + kept + middle:
        copy.wait_send()


def expand(fin, out, OUT, sem):
    copies = []
    for s in range(3):
        for z in range(4):
            m = [fin[i, z] for i in range(3)]
            base = fin[3 + s, z]
            for q in range(19):
                v = plus(base, along(q, m))
                OUT[19 * s + q, z] = v + fin[6 + q, z] if s == 2 else v
        part = pl.ds(19 * s, 19)
        copies.append(pltpu.make_async_copy(OUT.at[part], out.at[part], sem.at[s]))
        copies[s].start()
    for copy in copies:
        copy.wait()


N_REMOTE = 6 + 8 + 16 + 6 + 8 + 6 + 16 + 6 + 8


def block(size_x, size_y, *args):
    def vmem(*shape, dtype=F32):
        return pltpu.VMEM(shape, dtype)

    bf = jnp.bfloat16
    scratch = [
        vmem(57, 4, 8, 128),
        vmem(57, 4, 8, 128, dtype=bf),
        vmem(57, 4, 8, 128, dtype=bf),
        vmem(3, 4, 8, 128, dtype=bf),
        vmem(3, 4, 8, 128, dtype=bf),
        vmem(3, 19, 64, 128),
        vmem(9, 48, 128),
        vmem(9, 48, 128),
        vmem(6, 80, 128),
        vmem(19, 64, 128),
        vmem(13, 8, 128),
        vmem(13, 16, 128),
        vmem(13, 16, 128),
        vmem(3, 8, 128),
        vmem(3, 16, 128),
        vmem(3, 16, 128),
        vmem(1, 8, 128),
        vmem(1, 16, 128),
        vmem(1, 16, 128),
        vmem(57, 8, 128),
        vmem(19, 8, 128),
        vmem(9, 8, 128),
        vmem(9, 8, 128),
        vmem(6, 96, 128),
        vmem(6, 3, 24, 128),
        vmem(9, 7, 8, 128),
        vmem(3, 7, 8, 128),
        vmem(18, 96, 128),
        vmem(18, 3, 24, 128),
        vmem(6, 48, 128),
        vmem(6, 24, 128),
        vmem(6, 3, 24, 128),
        vmem(19, 24, 128),
        pltpu.SemaphoreType.DMA((5,)),
        pltpu.SemaphoreType.DMA((N_REMOTE,)),
        pltpu.SemaphoreType.DMA((N_REMOTE,)),
    ]
    fin = pl.pallas_call(
        lambda *refs: kernel(size_x, size_y, *refs),
        out_shape=jax.ShapeDtypeStruct((25, 4, 8, 128), F32),
        in_specs=[pl.BlockSpec(memory_space=pltpu.HBM)] * 5,
        out_specs=pl.BlockSpec(memory_space=pltpu.VMEM),
        scratch_shapes=scratch,
        compiler_params=pltpu.CompilerParams(
            collective_id=0, has_side_effects=True, vmem_limit_bytes=24 << 20
        ),
        name="lattice_adjoint",
    )(*[pltpu.with_memory_space_constraint(a, pltpu.HBM) for a in args])
    return pl.pallas_call(
        expand,
        out_shape=jax.ShapeDtypeStruct((57, 4, 8, 128), F32),
        in_specs=[pl.BlockSpec(memory_space=pltpu.VMEM)],
        out_specs=pl.BlockSpec(memory_space=pltpu.HBM),
        scratch_shapes=[vmem(57, 4, 8, 128), pltpu.SemaphoreType.DMA((3,))],
        compiler_params=pltpu.CompilerParams(vmem_limit_bytes=8 << 20),
        name="lattice_expand",
    )(fin)


def solution(mesh):
    size_x, size_y = mesh.shape["gx"], mesh.shape["gy"]
    spec = P(None, None, "gx", "gy")
    return jax.shard_map(
        lambda *args: block(size_x, size_y, *args),
        mesh=mesh,
        in_specs=(spec,) * 5,
        out_specs=spec,
        check_vma=False,
    )
```

```python
import math

import jax
import jax.numpy as jnp
from jax import lax
from jax.experimental import pallas as pl
from jax.experimental.pallas import tpu as pltpu
from jax.sharding import PartitionSpec as P

MESH = pl.DeviceIdType.MESH
VELOCITY = (
    (1, 0, 0),
    (-1, 0, 0),
    (0, 1, 0),
    (0, -1, 0),
    (1, 1, 0),
    (-1, -1, 0),
    (1, -1, 0),
    (-1, 1, 0),
    (1, 0, 1),
    (-1, 0, -1),
    (1, 0, -1),
    (-1, 0, 1),
    (0, 1, 1),
    (0, -1, -1),
    (0, 1, -1),
    (0, -1, 1),
    (0, 0, 0),
    (0, 0, 1),
    (0, 0, -1),
)
TAU = (1.0, 1.0, 1.25)
G = ((0.0, 1.2, -0.6), (1.2, 0.0, -0.6), (-0.6, -0.6, -0.3))
ORDER = (1, 5, 7, 9, 11, 2, 3, 12, 13, 14, 15, 16, 17, 18, 0, 4, 6, 8, 10)
SLOT = {q: i for i, q in enumerate(ORDER)}
F32 = jnp.float32
N_SETS = 5


def up_y(v):
    return pltpu.roll(v, 127, 1)


def dn_y(v):
    return pltpu.roll(v, 1, 1)


def shift_y(v, cy):
    return v if cy == 0 else (up_y(v) if cy == 1 else dn_y(v))


def near(ld, f):
    n = dict(
        c=ld(f, 0, 0),
        xp=ld(f, 1, 0),
        xm=ld(f, -1, 0),
        zp=ld(f, 0, 1),
        zm=ld(f, 0, -1),
        pp=ld(f, 1, 1),
        pm=ld(f, 1, -1),
        mp=ld(f, -1, 1),
        mm=ld(f, -1, -1),
    )
    n["dx"] = n["xp"] - n["xm"]
    n["dz"] = n["zp"] - n["zm"]
    n["sx"] = n["xp"] + n["xm"]
    n["sz"] = n["zp"] + n["zm"]
    return n


def corner(n):
    return (n["pp"] + n["mm"]) + (n["pm"] + n["mp"])


def cross(n):
    return (n["pp"] + n["mm"]) - (n["pm"] + n["mp"])


def corner_x(n):
    return (n["pp"] - n["mm"]) + (n["pm"] - n["mp"])


def corner_z(n):
    return (n["pp"] - n["mm"]) - (n["pm"] - n["mp"])


def gradient(n):
    h = 2.0 * n["c"] + n["sx"] + n["sz"]
    r = dict(
        hp=up_y(h),
        hm=dn_y(h),
        dxp=up_y(n["dx"]),
        dxm=dn_y(n["dx"]),
        dzp=up_y(n["dz"]),
        dzm=dn_y(n["dz"]),
    )
    gx = 2.0 * n["dx"] + corner_x(n) + (r["dxp"] + r["dxm"])
    gz = 2.0 * n["dz"] + corner_z(n) + (r["dzp"] + r["dzm"])
    return (gx, r["hp"] - r["hm"], gz), r


def second(sx, sz, cor, crs, r):
    xx = 2.0 * sx + cor + (up_y(sx) + dn_y(sx))
    zz = 2.0 * sz + cor + (up_y(sz) + dn_y(sz))
    return dict(
        xx=xx,
        yy=r["hp"] + r["hm"],
        zz=zz,
        xy=r["dxp"] - r["dxm"],
        yz=r["dzp"] - r["dzm"],
        xz=crs,
    )


def vector_stencil(nx, ny, nz):
    px = 2.0 * nx["sx"] + corner(nx) + cross(nz)
    px = px + up_y(nx["sx"] + ny["dx"]) + dn_y(nx["sx"] - ny["dx"])
    pz = 2.0 * nz["sz"] + corner(nz) + cross(nx)
    pz = pz + up_y(nz["sz"] + ny["dz"]) + dn_y(nz["sz"] - ny["dz"])
    a = 2.0 * ny["c"] + ny["sx"] + ny["sz"]
    b = nx["dx"] + nz["dz"]
    return px, up_y(a + b) + dn_y(a - b), pz


def divergence(nx, ny, nz):
    u = nx["dx"] + nz["dz"]
    v = 2.0 * ny["c"] + ny["sx"] + ny["sz"]
    return 2.0 * u + corner_x(nx) + corner_z(nz) + up_y(u + v) + dn_y(u - v)


def moments_of(g):
    p = {}
    m = {}
    for q in (0, 2, 4, 6, 8, 10, 12, 14, 17):
        p[q] = g[q] + g[q + 1]
        m[q] = g[q] - g[q + 1]
    xy, xz, yz = p[4] + p[6], p[8] + p[10], p[12] + p[14]
    ax, ay, az = 2.0 * p[0], 2.0 * p[2], 2.0 * p[17]
    a = 12.0 * g[16] + (ax + ay + az) + (xy + xz + yz)
    b = (
        2.0 * m[0] + (m[4] + m[6]) + (m[8] + m[10]),
        2.0 * m[2] + (m[4] - m[6]) + (m[12] + m[14]),
        2.0 * m[17] + (m[8] - m[10]) + (m[12] - m[14]),
    )
    c = dict(
        xx=ax + xy + xz,
        yy=ay + xy + yz,
        zz=az + xz + yz,
        xy=p[4] - p[6],
        xz=p[8] - p[10],
        yz=p[12] - p[14],
    )
    return a, b, c


def pick_potentials(rho, d):
    psi = [1.0 - jnp.exp(-r) for r in rho]
    mixed = [
        1.2 * psi[1] - 0.6 * psi[2],
        1.2 * psi[0] - 0.6 * psi[2],
        -0.6 * (psi[0] + psi[1]) - 0.3 * psi[2],
    ]
    return psi, mixed + [d[j] * psi[2] for j in range(3)]


def thrusts(ld, d):
    grads, rolled, sums = [], [], []
    for s in range(3):
        n = near(ld, s)
        g, r = gradient(n)
        grads.append(g)
        if s < 2:
            rolled.append(r)
            sums.append((n["sx"], n["sz"], corner(n), cross(n)))
    diff = [b - a for a, b in zip(*sums)]
    r = {key: rolled[1][key] - rolled[0][key] for key in rolled[0]}
    m = second(*diff, r)
    e = [near(ld, 3 + j) for j in range(3)]
    p = vector_stencil(*e)
    k = 1.0 / 36.0
    k2 = 1.0 / (36.0 * 1.2)
    turned = (
        m["xx"] * d[0] + m["xy"] * d[1] + m["xz"] * d[2],
        m["xy"] * d[0] + m["yy"] * d[1] + m["yz"] * d[2],
        m["xz"] * d[0] + m["yz"] * d[1] + m["zz"] * d[2],
    )
    t0 = [-k * (grads[0][i] + p[i]) for i in range(3)]
    t1 = [k * (p[i] - grads[1][i]) for i in range(3)]
    t2 = [k2 * turned[i] - k * grads[2][i] for i in range(3)]
    return t0 + t1 + t2


def local_adjoint(mom, rho, u, psi, t, d):
    x, e_val, wt, ratio = [], [], [], []
    m = [None] * 3
    for s in range(3):
        a, b, c = mom[s]
        ratio.append(TAU[s] * psi[s] / rho[s])
        ts = t[3 * s : 3 * s + 3]
        v = [u[i] + ratio[s] * ts[i] for i in range(3)]
        cv = (
            c["xx"] * v[0] + c["xy"] * v[1] + c["xz"] * v[2],
            c["xy"] * v[0] + c["yy"] * v[1] + c["yz"] * v[2],
            c["xz"] * v[0] + c["yz"] * v[1] + c["zz"] * v[2],
        )
        k = 1.0 / (36.0 * TAU[s])
        b3 = [3.0 * b[i] for i in range(3)]
        a3 = 3.0 * a
        w = [b3[i] + 9.0 * cv[i] - a3 * v[i] for i in range(3)]
        half = (b3[0] + w[0]) * v[0] + (b3[1] + w[1]) * v[1] + (b3[2] + w[2]) * v[2]
        e_val.append(k * a + (0.5 * k) * half)
        w = [k * w[i] for i in range(3)]
        wt.append(w[0] * ts[0] + w[1] * ts[1] + w[2] * ts[2])
        for i in range(3):
            term = rho[s] * w[i]
            m[i] = term if s == 0 else m[i] + term
        tp = TAU[s] * psi[s]
        x.extend(tp * w[i] for i in range(3))
    inverse = 1.0 / (rho[0] + rho[1] + rho[2])
    m = [m[i] * inverse for i in range(3)]
    mu = m[0] * u[0] + m[1] * u[1] + m[2] * u[2]
    dens = [e_val[s] + wt[s] * (TAU[s] * (1.0 - psi[s]) - ratio[s]) - mu for s in range(3)]
    y = x[6:9]
    kxx, kyy, kzz = y[0] * d[0], y[1] * d[1], y[2] * d[2]
    kept = [
        kxx,
        kyy,
        kzz,
        y[0] * d[1] + y[1] * d[0],
        y[0] * d[2] + y[2] * d[0],
        y[1] * d[2] + y[2] * d[1],
        kxx + kyy,
        kyy + kzz,
        kxx + kzz,
    ]
    return x + kept, m, dens


def spread(ld, dens, psi, d):
    n = [[near(ld, 3 * s + i) for i in range(3)] for s in range(3)]
    y = [divergence(*n[s]) for s in range(3)]
    diff = [{key: n[0][i][key] - n[1][i][key] for key in n[0][i]} for i in range(3)]
    z = vector_stencil(*diff)
    xx, zz, a3, kxz = near(ld, 9), near(ld, 11), near(ld, 17), near(ld, 13)
    a1, a2, kxy, kyz = near(ld, 15), near(ld, 16), near(ld, 12), near(ld, 14)
    u = 2.0 * ld(10, 0, 0) + a1["sx"] + a2["sz"]
    v = kxy["dx"] + kyz["dz"]
    quad = 2.0 * (xx["sx"] + zz["sz"]) + corner(a3) + cross(kxz) + up_y(u + v) + dn_y(u - v)
    k = 1.0 / 36.0
    back = [
        1.2 * y[1] - 0.6 * y[2] + quad,
        1.2 * y[0] - 0.6 * y[2] - quad,
        -0.6 * (y[0] + y[1]) - 0.3 * y[2] - (d[0] * z[0] + d[1] * z[1] + d[2] * z[2]),
    ]
    return [dens[s] + (k * (1.0 - psi[s])) * back[s] for s in range(3)]


def late_moments(ld, pulled):
    x, y, z = (near(ld, i) for i in range(3))
    axx, azz = 2.0 * x["dx"], 2.0 * z["dz"]
    ayy = 2.0 * (up_y(y["c"]) - dn_y(y["c"]))
    exz = corner_x(x) + corner_z(z)
    exy = up_y(x["dx"] + y["sx"]) + dn_y(x["dx"] - y["sx"])
    eyz = up_y(z["dz"] + y["sz"]) + dn_y(z["dz"] - y["sz"])
    a_m = (axx + ayy + azz) + (exy + exz + eyz)
    b_m = vector_stencil(x, y, z)
    c_m = dict(
        xx=axx + exy + exz,
        yy=ayy + exy + eyz,
        zz=azz + exz + eyz,
        xy=up_y(y["dx"] + x["sx"]) + dn_y(y["dx"] - x["sx"]),
        yz=up_y(y["dz"] + z["sz"]) + dn_y(y["dz"] - z["sz"]),
        xz=corner_z(x) + corner_x(z),
    )
    extra = moments_of(pulled)
    out = []
    for s in range(3):
        n = near(ld, 3 + s)
        g, r = gradient(n)
        c = second(n["sx"], n["sz"], corner(n), cross(n), r)
        a = 12.0 * n["c"] + 2.0 * (n["sx"] + n["sz"]) + corner(n) + c["yy"] + a_m
        b = [g[i] + b_m[i] for i in range(3)]
        c = {key: c[key] + c_m[key] for key in c}
        if s == 2:
            a = a + 0.2 * extra[0]
            b = [b[i] + 0.2 * extra[1][i] for i in range(3)]
            c = {key: c[key] + 0.2 * extra[2][key] for key in c}
        out.append((a, b, c))
    return out


def along(q, m):
    out = None
    for i in range(3):
        c = VELOCITY[q][i]
        if c != 0:
            term = m[i] if c > 0 else -m[i]
            out = term if out is None else out + term
    return out

def plus(base, term):
    return base if term is None else base + term


def kernel(
    size_x,
    size_y,
    a_in,
    pe_in,
    pl_in,
    de_in,
    dl_in,
    FIN,
    A,
    NE,
    NL,
    DE,
    DL,
    F,
    FL,
    FE,
    FM,
    FG,
    PO,
    PLX,
    PRX,
    PGO,
    PGL,
    PGR,
    PMO,
    PML,
    PMR,
    SA,
    SG,
    SL,
    SE,
    QM,
    QS,
    TB,
    SI,
    XM,
    XS,
    LM,
    LS,
    MS,
    TS,
    W,
    lsem,
    ssem,
    rsem,
):
    gx, gy = lax.axis_index("gx"), lax.axis_index("gy")
    xu, xd = lax.rem(gx + 1, size_x), lax.rem(gx + size_x - 1, size_x)
    yr, yl = lax.rem(gy + 1, size_y), lax.rem(gy + size_y - 1, size_y)
    everyone = [(xu, gy), (xd, gy), (gx, yr), (gx, yl), (xu, yr), (xu, yl), (xd, yr), (xd, yl)]
    barrier = pltpu.get_barrier_semaphore()
    for who in everyone:
        pl.semaphore_signal(barrier, inc=1, device_id=who, device_id_type=MESH)
    loads = [
        pltpu.make_async_copy(src, dst, lsem.at[i])
        for i, (src, dst) in enumerate(
            ((pl_in, NL), (dl_in, DL), (a_in, A), (pe_in, NE), (de_in, DE))
        )
    ]
    for copy in loads:
        copy.start()

    lane = lax.broadcasted_iota(jnp.int32, (8, 128), 1)
    sub = lax.broadcasted_iota(jnp.int32, (8, 128), 0)
    c16 = lane % 16
    group16 = lane // 16
    group4 = lane // 4

    current = [0]
    sent = [0] * N_SETS

    def remote(src, dst, who):
        sent[current[0]] += math.prod(src.shape) // 128
        return pltpu.make_async_remote_copy(
            src_ref=src,
            dst_ref=dst,
            send_sem=ssem.at[0],
            recv_sem=rsem.at[current[0]],
            device_id=who,
            device_id_type=MESH,
        )

    def begin(copies):
        for copy in copies:
            copy.start()
        current[0] += 1
        return current[0] - 1

    def wait_rows(rows, sem):
        span = W.at[pl.ds(0, rows)]
        pltpu.make_async_copy(span, span, sem).wait()

    def arrive(number):
        wait_rows(sent[number], rsem.at[number])

    def row_copies(ref, lead, base, depth, up, down):
        out = []
        for z in range(4):
            row = base + 12 * z
            if up:
                out.append(
                    remote(
                        ref.at[lead + (pl.ds(row + 10 - depth, depth),)],
                        ref.at[lead + (pl.ds(row + 2 - depth, depth),)],
                        (xu, gy),
                    )
                )
            if down:
                out.append(
                    remote(
                        ref.at[lead + (pl.ds(row + 2, depth),)],
                        ref.at[lead + (pl.ds(row + 10, depth),)],
                        (xd, gy),
                    )
                )
        return out

    def pop_rows(ref, lead, base):
        return (
            row_copies(ref, lead + (pl.ds(0, 5),), base, 2, True, False)
            + row_copies(ref, lead + (pl.ds(14, 5),), base, 2, False, True)
            + row_copies(ref, lead + (pl.ds(5, 9),), base, 1, True, True)
        )

    def edge_copies(own, left, right, tiles):
        out = []
        for who, ref, src, dst in (
            ((xu, yr), left, (6, 2), 2),
            ((xd, yr), left, (0, 2), 12),
            ((xu, yl), right, (6, 2), 2),
            ((xd, yl), right, (0, 2), 12),
            ((gx, yr), left, (0, 8), 4),
            ((gx, yl), right, (0, 8), 4),
        ):
            out.append(
                remote(
                    own.at[tiles, pl.ds(*src)],
                    ref.at[tiles, pl.ds(dst, src[1])],
                    who,
                )
            )
        return out

    def pack(acc, v, z, slot):
        moved = pltpu.roll(v, (32 * z + 4 * slot + 2) % 128, 1)
        return moved if acc is None else jnp.where(group4 == 8 * z + slot, moved, acc)

    def strip_of(own, cy, left, right, slot):
        acc = None
        for z in range(4):
            for h in range(2):
                v = own(z, h)
                base = 32 * z + 16 * h
                w = jnp.where(
                    c16 < 8,
                    pltpu.roll(v, (base - 122 - cy) % 128, 1),
                    pltpu.roll(v, (base + 10 - cy) % 128, 1),
                )
                acc = w if acc is None else jnp.where(group16 == 2 * z + h, w, acc)
        odd = group16 % 2 == 1
        if cy >= 0 or True:
            r = [pltpu.roll(right(h), (16 * h + 4 - cy - 4 * slot) % 128, 1) for h in range(2)]
            r = jnp.where(odd, r[1], r[0])
            acc = jnp.where((c16 >= 6 - cy) & (c16 < 8), r, acc)
        l = [pltpu.roll(left(h), (16 * h + 8 - cy - 4 * slot) % 128, 1) for h in range(2)]
        l = jnp.where(odd, l[1], l[0])
        return jnp.where((c16 >= 8) & (c16 <= 9 - cy), l, acc)

    def store_strip(ref, f, v):
        ref[f, 1, 8:16, :] = v
        ref[f, 0, 8:16, :] = pltpu.roll(v, 32, 1)
        ref[f, 2, 8:16, :] = pltpu.roll(v, 96, 1)

    def strip_loader(ref):
        return lambda f, dx, dz: ref[f, 1 + dz, 8 + dx : 16 + dx, :]

    def flat_loader(ref, k):
        return lambda f, dx, dz: ref[f, pl.ds(8 * k + (16 + dx + 12 * dz), 8), :]

    def over_tiles(body):
        lax.fori_loop(0, 6, lambda k, carry: (body(k), carry)[1], 0, unroll=3)

    def saved(pops, dips, ref, tile0):
        acc = [None, None]
        for z in range(4):
            flow = [None] * 19
            dens = []
            for s in range(3):
                total = None
                for q in range(19):
                    f = pops[19 * s + q, z].astype(F32)
                    total = f if total is None else total + f
                    flow[q] = f if s == 0 else flow[q] + f
                dens.append(total)
            inverse = 1.0 / (dens[0] + dens[1] + dens[2])
            fields = list(dens)
            for i in range(3):
                amount = None
                for q in range(19):
                    c = VELOCITY[q][i]
                    if c != 0:
                        term = flow[q] if c > 0 else -flow[q]
                        amount = term if amount is None else amount + term
                fields.append(amount * inverse)
            fields.extend(dips[i, z].astype(F32) for i in range(3))
            for f in range(9):
                ref[f, 12 * z + 2 : 12 * z + 10, :] = fields[f]
                acc[f // 8] = pack(acc[f // 8], fields[f], z, f % 8)
        PO[tile0] = acc[0]
        PO[tile0 + 1] = acc[1]

    loads[0].wait()
    loads[1].wait()
    saved(NL, DL, FL, 9)

    loads[2].wait()

    def spread_pops(s, carry):
        acc = [None] * 3
        for o, q in enumerate(ORDER):
            for z in range(4):
                v = A[19 * s + q, (z + VELOCITY[q][2]) % 4]
                F[s, o, 8 + 12 * z + 2 : 8 + 12 * z + 10, :] = v
                acc[o // 8] = pack(acc[o // 8], v, z, o % 8)
        for i in range(3):
            PO[3 * s + i] = acc[i]
        return carry

    lax.fori_loop(0, 3, spread_pops, 0)

    pl.semaphore_wait(barrier, 8)
    every = (pl.ds(0, 9),)
    first = edge_copies(PO, PLX, PRX, pl.ds(0, 11))
    first += row_copies(FL, every, 0, 2, True, True)
    first = begin(first)
    rows = begin(pop_rows(F, (pl.ds(0, 3),), 8))

    loads[3].wait()
    loads[4].wait()
    saved(NE, DE, FE, 11)
    second_set = begin(
        edge_copies(PO, PLX, PRX, pl.ds(11, 2)) + row_copies(FE, every, 0, 2, True, True)
    )

    def potentials(ref, strips):
        def body(k):
            rows = pl.ds(8 * k, 8)
            psi, fields = pick_potentials(
                [ref[s, rows, :] for s in range(3)], [ref[6 + i, rows, :] for i in range(3)]
            )
            for s in range(3):
                SI[s, k] = psi[s]
            for f in range(6):
                QM[f, pl.ds(16 + 8 * k, 8), :] = fields[f]
                QM[f, pl.ds(lax.rem(8 * k + 64, 96), 8), :] = fields[f]

        over_tiles(body)
        psi, fields = pick_potentials(
            [strips[s] for s in range(3)], [strips[6 + i] for i in range(3)]
        )
        for s in range(3):
            SI[s, 6] = psi[s]
        for f in range(6):
            store_strip(QS, f, fields[f])

    def all_thrusts(ref, strips):
        def body(k):
            rows = pl.ds(8 * k, 8)
            t = thrusts(flat_loader(QM, k), [ref[6 + i, rows, :] for i in range(3)])
            for f in range(9):
                TB[f, k] = t[f]

        over_tiles(body)
        t = thrusts(strip_loader(QS), [strips[6 + i] for i in range(3)])
        for f in range(9):
            TB[f, 6] = t[f]

    def field_strips(ref, strips, tile0):
        for f in range(9):
            tile, slot = tile0 + f // 8, f % 8
            strips[f] = strip_of(
                lambda z, h: ref[f, 12 * z + 4 * h : 12 * z + 4 * h + 8, :],
                0,
                lambda h: PLX[tile, 2 + 4 * h : 10 + 4 * h, :],
                lambda h: PRX[tile, 2 + 4 * h : 10 + 4 * h, :],
                slot,
            )

    def adjoint_stage(ref, strips, main_moments, strip_moments):
        def one(mom, k, rho, u, d, put_x, put_l):
            psi = [SI[s, k] for s in range(3)]
            t = [TB[f, k] for f in range(9)]
            fields, m, dens = local_adjoint(mom, rho, u, psi, t, d)
            for f in range(18):
                put_x(f, fields[f])
            for i in range(3):
                put_l(i, m[i])
                put_l(3 + i, dens[i])

        def body(k):
            rows = pl.ds(8 * k, 8)

            def put_x(f, v):
                XM[f, pl.ds(16 + 8 * k, 8), :] = v
                XM[f, pl.ds(lax.rem(8 * k + 64, 96), 8), :] = v

            def put_l(f, v):
                LM[f, rows, :] = v

            get = [ref[f, rows, :] for f in range(9)]
            one(main_moments(k), k, get[0:3], get[3:6], get[6:9], put_x, put_l)

        over_tiles(body)

        def put_x(f, v):
            store_strip(XS, f, v)

        def put_l(f, v):
            LS[f, 8:16, :] = v

        get = [strips[f] for f in range(9)]
        one(strip_moments(), 6, get[0:3], get[3:6], get[6:9], put_x, put_l)

    def spread_stage(ref, strips):
        def body(k):
            rows = pl.ds(8 * k, 8)
            new = spread(
                flat_loader(XM, k),
                [LM[3 + s, rows, :] for s in range(3)],
                [SI[s, k] for s in range(3)],
                [ref[6 + i, rows, :] for i in range(3)],
            )
            for s in range(3):
                LM[3 + s, rows, :] = new[s]

        over_tiles(body)
        new = spread(
            strip_loader(XS),
            [LS[3 + s, 8:16, :] for s in range(3)],
            [SI[s, 6] for s in range(3)],
            [strips[6 + i] for i in range(3)],
        )
        for s in range(3):
            LS[3 + s, 8:16, :] = new[s]

    def folded(ref, f):
        low = ref[f, 10:18, :]
        high = pltpu.roll(ref[f, 6:14, :], 112, 1)
        return jnp.where(sub < 4, low, high)

    def with_edges(v, edge, z):
        right = pltpu.roll(edge, (122 - 32 * z) % 128, 1)
        left = pltpu.roll(edge, (-32 * z - 10) % 128, 1)
        return jnp.where(lane >= 126, right, jnp.where(lane < 2, left, v))

    arrive(first)
    field_strips(FL, SL, 9)
    potentials(FL, SL)
    all_thrusts(FL, SL)
    arrive(rows)

    acc = [None] * 3
    for o, q in enumerate(ORDER):
        cx, cy, cz = VELOCITY[q]
        tile, slot = 6 + o // 8, o % 8
        for z in range(4):
            v = shift_y(F[2, o, 8 + 12 * z + 2 + cx : 8 + 12 * z + 10 + cx, :], cy)
            if cy == -1:
                halo = pltpu.roll(
                    PLX[tile, 4 + cx : 12 + cx, :], (-(32 * z + 4 * slot + 1)) % 128, 1
                )
                v = jnp.where(lane == 0, halo, v)
            if cy == 1:
                halo = pltpu.roll(
                    PRX[tile, 4 + cx : 12 + cx, :], (127 - (32 * z + 4 * slot + 2)) % 128, 1
                )
                v = jnp.where(lane == 127, halo, v)
            to = (z - cz) % 4
            FG[o, 8 + 12 * to + 2 : 8 + 12 * to + 10, :] = v
            acc[o // 8] = pack(acc[o // 8], v, to, slot)
    for i in range(3):
        PGO[i] = acc[i]
    kept = begin(
        edge_copies(PGO, PGL, PGR, pl.ds(0, 3))
        + row_copies(FG, (pl.ds(0, 14),), 8, 2, True, False)
        + row_copies(FG, (pl.ds(5, 14),), 8, 2, False, True)
    )

    def pop_strips(s, carry):
        for o, q in enumerate(ORDER):
            cx, cy, _ = VELOCITY[q]
            SA[19 * s + o] = strip_of(
                lambda z, h: F[
                    s, o, 8 + 12 * z + 4 * h + cx : 8 + 12 * z + 4 * h + cx + 8, :
                ],
                cy,
                lambda h: PLX[3 * s + o // 8, 2 + 4 * h + cx : 10 + 4 * h + cx, :],
                lambda h: PRX[3 * s + o // 8, 2 + 4 * h + cx : 10 + 4 * h + cx, :],
                o % 8,
            )
        return carry

    lax.fori_loop(0, 3, pop_strips, 0)

    def pulled_moments(k):
        out = []
        for s in range(3):
            g = {}
            for o, q in enumerate(ORDER):
                cx, cy, _ = VELOCITY[q]
                g[q] = shift_y(F[s, o, pl.ds(8 * k + (8 + cx), 8), :], cy)
            out.append(moments_of(g))
        return out

    def pulled_strip_moments():
        return [moments_of({q: SA[19 * s + SLOT[q]] for q in range(19)}) for s in range(3)]

    adjoint_stage(FL, SL, pulled_moments, pulled_strip_moments)
    spread_stage(FL, SL)

    acc = None
    for f in range(6):
        edge = folded(LS, f)
        for z in range(4):
            v = with_edges(LM[f, 12 * z + 2 : 12 * z + 10, :], edge, z)
            FM[f, 16 + 12 * z + 2 : 16 + 12 * z + 10, :] = v
            acc = pack(acc, v, z, f)
    PMO[0] = acc
    middle = begin(
        edge_copies(PMO, PML, PMR, pl.ds(0, 1))
        + row_copies(FM, (pl.ds(0, 6),), 16, 2, True, True)
    )

    arrive(second_set)
    field_strips(FE, SE, 11)
    potentials(FE, SE)
    all_thrusts(FE, SE)

    arrive(kept)
    for o, q in enumerate(ORDER):
        cx, cy, _ = VELOCITY[q]
        SG[o] = strip_of(
            lambda z, h: FG[o, 8 + 12 * z + 4 * h + cx : 8 + 12 * z + 4 * h + cx + 8, :],
            cy,
            lambda h: PGL[o // 8, 2 + 4 * h + cx : 10 + 4 * h + cx, :],
            lambda h: PGR[o // 8, 2 + 4 * h + cx : 10 + 4 * h + cx, :],
            o % 8,
        )

    arrive(middle)
    for f in range(6):
        FM[f, 0:16, :] = FM[f, 48:64, :]
        FM[f, 64:80, :] = FM[f, 16:32, :]
        store_strip(
            MS,
            f,
            strip_of(
                lambda z, h: FM[f, 16 + 12 * z + 4 * h : 16 + 12 * z + 4 * h + 8, :],
                0,
                lambda h: PML[0, 2 + 4 * h : 10 + 4 * h, :],
                lambda h: PMR[0, 2 + 4 * h : 10 + 4 * h, :],
                f,
            ),
        )

    def middle_moments(k):
        g = {}
        for o, q in enumerate(ORDER):
            cx, cy, _ = VELOCITY[q]
            g[q] = shift_y(FG[o, pl.ds(8 * k + (8 + cx), 8), :], cy)
        return late_moments(flat_loader(FM, k), g)

    def middle_strip_moments():
        return late_moments(strip_loader(MS), {q: SG[SLOT[q]] for q in range(19)})

    adjoint_stage(FE, SE, middle_moments, middle_strip_moments)
    spread_stage(FE, SE)

    strip = strip_loader(MS)
    for o, q in enumerate(ORDER):
        cx, cy, cz = VELOCITY[q]
        if cy != 0:
            v = plus(strip(5, cx, cz), along(q, [strip(i, cx, cz) for i in range(3)]))
            TS[o, 8:16, :] = shift_y(v, cy) + 0.2 * SG[o]

    edges = [folded(LS, f) for f in range(6)]
    for z in range(4):
        for f in range(6):
            FIN[f, z] = with_edges(LM[f, 12 * z + 2 : 12 * z + 10, :], edges[f], z)
        for o, q in enumerate(ORDER):
            cx, cy, cz = VELOCITY[q]
            row = 12 * z + 2 + cx
            mid = [FM[i, 16 + row + 12 * cz : 24 + row + 12 * cz, :] for i in (0, 1, 2, 5)]
            v = plus(mid[3], along(q, mid[0:3])) + 0.2 * FG[o, 8 + row : 16 + row, :]
            v = shift_y(v, cy)
            if cy != 0:
                v = with_edges(v, folded(TS, o), z)
            FIN[6 + q, z] = 0.2 * v

    wait_rows(sum(sent), ssem.at[0])


def expand(fin, out, OUT, sem):
    copies = []
    for s in range(3):
        for z in range(4):
            m = [fin[i, z] for i in range(3)]
            base = fin[3 + s, z]
            for q in range(19):
                v = plus(base, along(q, m))
                OUT[19 * s + q, z] = v + fin[6 + q, z] if s == 2 else v
        part = pl.ds(19 * s, 19)
        copies.append(pltpu.make_async_copy(OUT.at[part], out.at[part], sem.at[s]))
        copies[s].start()
    for copy in copies:
        copy.wait()


def block(size_x, size_y, *args):
    def vmem(*shape, dtype=F32):
        return pltpu.VMEM(shape, dtype)

    bf = jnp.bfloat16
    scratch = [
        vmem(57, 4, 8, 128),
        vmem(57, 4, 8, 128, dtype=bf),
        vmem(57, 4, 8, 128, dtype=bf),
        vmem(3, 4, 8, 128, dtype=bf),
        vmem(3, 4, 8, 128, dtype=bf),
        vmem(3, 19, 64, 128),
        vmem(9, 48, 128),
        vmem(9, 48, 128),
        vmem(6, 80, 128),
        vmem(19, 64, 128),
        vmem(13, 8, 128),
        vmem(13, 16, 128),
        vmem(13, 16, 128),
        vmem(3, 8, 128),
        vmem(3, 16, 128),
        vmem(3, 16, 128),
        vmem(1, 8, 128),
        vmem(1, 16, 128),
        vmem(1, 16, 128),
        vmem(57, 8, 128),
        vmem(19, 8, 128),
        vmem(9, 8, 128),
        vmem(9, 8, 128),
        vmem(6, 96, 128),
        vmem(6, 3, 24, 128),
        vmem(9, 7, 8, 128),
        vmem(3, 7, 8, 128),
        vmem(18, 96, 128),
        vmem(18, 3, 24, 128),
        vmem(6, 48, 128),
        vmem(6, 24, 128),
        vmem(6, 3, 24, 128),
        vmem(19, 24, 128),
        vmem(3072, 128),
        pltpu.SemaphoreType.DMA((5,)),
        pltpu.SemaphoreType.DMA((1,)),
        pltpu.SemaphoreType.DMA((N_SETS,)),
    ]
    fin = pl.pallas_call(
        lambda *refs: kernel(size_x, size_y, *refs),
        out_shape=jax.ShapeDtypeStruct((25, 4, 8, 128), F32),
        in_specs=[pl.BlockSpec(memory_space=pltpu.HBM)] * 5,
        out_specs=pl.BlockSpec(memory_space=pltpu.VMEM),
        scratch_shapes=scratch,
        compiler_params=pltpu.CompilerParams(
            collective_id=0, has_side_effects=True, vmem_limit_bytes=24 << 20
        ),
        name="lattice_adjoint",
    )(*[pltpu.with_memory_space_constraint(a, pltpu.HBM) for a in args])
    return pl.pallas_call(
        expand,
        out_shape=jax.ShapeDtypeStruct((57, 4, 8, 128), F32),
        in_specs=[pl.BlockSpec(memory_space=pltpu.VMEM)],
        out_specs=pl.BlockSpec(memory_space=pltpu.HBM),
        scratch_shapes=[vmem(57, 4, 8, 128), pltpu.SemaphoreType.DMA((3,))],
        compiler_params=pltpu.CompilerParams(vmem_limit_bytes=8 << 20),
        name="lattice_expand",
    )(fin)


def solution(mesh):
    size_x, size_y = mesh.shape["gx"], mesh.shape["gy"]
    spec = P(None, None, "gx", "gy")
    return jax.shard_map(
        lambda *args: block(size_x, size_y, *args),
        mesh=mesh,
        in_specs=(spec,) * 5,
        out_specs=spec,
        check_vma=False,
    )
```

```python
import math

import jax
import jax.numpy as jnp
from jax import lax
from jax.experimental import pallas as pl
from jax.experimental.pallas import tpu as pltpu
from jax.sharding import PartitionSpec as P

MESH = pl.DeviceIdType.MESH
VELOCITY = (
    (1, 0, 0),
    (-1, 0, 0),
    (0, 1, 0),
    (0, -1, 0),
    (1, 1, 0),
    (-1, -1, 0),
    (1, -1, 0),
    (-1, 1, 0),
    (1, 0, 1),
    (-1, 0, -1),
    (1, 0, -1),
    (-1, 0, 1),
    (0, 1, 1),
    (0, -1, -1),
    (0, 1, -1),
    (0, -1, 1),
    (0, 0, 0),
    (0, 0, 1),
    (0, 0, -1),
)
TAU = (1.0, 1.0, 1.25)
G = ((0.0, 1.2, -0.6), (1.2, 0.0, -0.6), (-0.6, -0.6, -0.3))
ORDER = (1, 5, 7, 9, 11, 2, 3, 12, 13, 14, 15, 16, 17, 18, 0, 4, 6, 8, 10)
SLOT = {q: i for i, q in enumerate(ORDER)}
RIGHTWARD = tuple(o for o, q in enumerate(ORDER) if VELOCITY[q][1] <= 0)
LEFTWARD = tuple(o for o, q in enumerate(ORDER) if VELOCITY[q][1] >= 0)
F32 = jnp.float32
N_SETS = 6


def up_y(v):
    return pltpu.roll(v, 127, 1)


def dn_y(v):
    return pltpu.roll(v, 1, 1)


def shift_y(v, cy):
    return v if cy == 0 else (up_y(v) if cy == 1 else dn_y(v))


def near(ld, f):
    n = dict(
        c=ld(f, 0, 0),
        xp=ld(f, 1, 0),
        xm=ld(f, -1, 0),
        zp=ld(f, 0, 1),
        zm=ld(f, 0, -1),
        pp=ld(f, 1, 1),
        pm=ld(f, 1, -1),
        mp=ld(f, -1, 1),
        mm=ld(f, -1, -1),
    )
    n["dx"] = n["xp"] - n["xm"]
    n["dz"] = n["zp"] - n["zm"]
    n["sx"] = n["xp"] + n["xm"]
    n["sz"] = n["zp"] + n["zm"]
    return n


def corner(n):
    return (n["pp"] + n["mm"]) + (n["pm"] + n["mp"])


def cross(n):
    return (n["pp"] + n["mm"]) - (n["pm"] + n["mp"])


def corner_x(n):
    return (n["pp"] - n["mm"]) + (n["pm"] - n["mp"])


def corner_z(n):
    return (n["pp"] - n["mm"]) - (n["pm"] - n["mp"])


def gradient(n):
    h = 2.0 * n["c"] + n["sx"] + n["sz"]
    r = dict(
        hp=up_y(h),
        hm=dn_y(h),
        dxp=up_y(n["dx"]),
        dxm=dn_y(n["dx"]),
        dzp=up_y(n["dz"]),
        dzm=dn_y(n["dz"]),
    )
    gx = 2.0 * n["dx"] + corner_x(n) + (r["dxp"] + r["dxm"])
    gz = 2.0 * n["dz"] + corner_z(n) + (r["dzp"] + r["dzm"])
    return (gx, r["hp"] - r["hm"], gz), r


def second(sx, sz, cor, crs, r):
    xx = 2.0 * sx + cor + (up_y(sx) + dn_y(sx))
    zz = 2.0 * sz + cor + (up_y(sz) + dn_y(sz))
    return dict(
        xx=xx,
        yy=r["hp"] + r["hm"],
        zz=zz,
        xy=r["dxp"] - r["dxm"],
        yz=r["dzp"] - r["dzm"],
        xz=crs,
    )


def vector_stencil(nx, ny, nz):
    px = 2.0 * nx["sx"] + corner(nx) + cross(nz)
    px = px + up_y(nx["sx"] + ny["dx"]) + dn_y(nx["sx"] - ny["dx"])
    pz = 2.0 * nz["sz"] + corner(nz) + cross(nx)
    pz = pz + up_y(nz["sz"] + ny["dz"]) + dn_y(nz["sz"] - ny["dz"])
    a = 2.0 * ny["c"] + ny["sx"] + ny["sz"]
    b = nx["dx"] + nz["dz"]
    return px, up_y(a + b) + dn_y(a - b), pz


def divergence(nx, ny, nz):
    u = nx["dx"] + nz["dz"]
    v = 2.0 * ny["c"] + ny["sx"] + ny["sz"]
    return 2.0 * u + corner_x(nx) + corner_z(nz) + up_y(u + v) + dn_y(u - v)


def moments_of(g):
    p = {}
    m = {}
    for q in (0, 2, 4, 6, 8, 10, 12, 14, 17):
        p[q] = g[q] + g[q + 1]
        m[q] = g[q] - g[q + 1]
    xy, xz, yz = p[4] + p[6], p[8] + p[10], p[12] + p[14]
    ax, ay, az = 2.0 * p[0], 2.0 * p[2], 2.0 * p[17]
    a = 12.0 * g[16] + (ax + ay + az) + (xy + xz + yz)
    b = (
        2.0 * m[0] + (m[4] + m[6]) + (m[8] + m[10]),
        2.0 * m[2] + (m[4] - m[6]) + (m[12] + m[14]),
        2.0 * m[17] + (m[8] - m[10]) + (m[12] - m[14]),
    )
    c = dict(
        xx=ax + xy + xz,
        yy=ay + xy + yz,
        zz=az + xz + yz,
        xy=p[4] - p[6],
        xz=p[8] - p[10],
        yz=p[12] - p[14],
    )
    return a, b, c


def pick_potentials(rho, d):
    psi = [1.0 - jnp.exp(-r) for r in rho]
    mixed = [
        1.2 * psi[1] - 0.6 * psi[2],
        1.2 * psi[0] - 0.6 * psi[2],
        -0.6 * (psi[0] + psi[1]) - 0.3 * psi[2],
    ]
    return psi, mixed + [d[j] * psi[2] for j in range(3)]


def thrusts(ld, d):
    grads, rolled, sums = [], [], []
    for s in range(3):
        n = near(ld, s)
        g, r = gradient(n)
        grads.append(g)
        if s < 2:
            rolled.append(r)
            sums.append((n["sx"], n["sz"], corner(n), cross(n)))
    diff = [b - a for a, b in zip(*sums)]
    r = {key: rolled[1][key] - rolled[0][key] for key in rolled[0]}
    m = second(*diff, r)
    e = [near(ld, 3 + j) for j in range(3)]
    p = vector_stencil(*e)
    k = 1.0 / 36.0
    k2 = 1.0 / (36.0 * 1.2)
    turned = (
        m["xx"] * d[0] + m["xy"] * d[1] + m["xz"] * d[2],
        m["xy"] * d[0] + m["yy"] * d[1] + m["yz"] * d[2],
        m["xz"] * d[0] + m["yz"] * d[1] + m["zz"] * d[2],
    )
    t0 = [-k * (grads[0][i] + p[i]) for i in range(3)]
    t1 = [k * (p[i] - grads[1][i]) for i in range(3)]
    t2 = [k2 * turned[i] - k * grads[2][i] for i in range(3)]
    return t0 + t1 + t2


def local_adjoint(mom, rho, u, psi, t, velocity, ratio, inverse):
    x, e_val, wt = [], [], []
    m = [None] * 3
    for s in range(3):
        a, b, c = mom[s]
        ts = t[3 * s : 3 * s + 3]
        v = velocity[3 * s : 3 * s + 3]
        cv = (
            c["xx"] * v[0] + c["xy"] * v[1] + c["xz"] * v[2],
            c["xy"] * v[0] + c["yy"] * v[1] + c["yz"] * v[2],
            c["xz"] * v[0] + c["yz"] * v[1] + c["zz"] * v[2],
        )
        k = 1.0 / (36.0 * TAU[s])
        b3 = [3.0 * b[i] for i in range(3)]
        a3 = 3.0 * a
        w = [b3[i] + 9.0 * cv[i] - a3 * v[i] for i in range(3)]
        half = (b3[0] + w[0]) * v[0] + (b3[1] + w[1]) * v[1] + (b3[2] + w[2]) * v[2]
        e_val.append(k * a + (0.5 * k) * half)
        w = [k * w[i] for i in range(3)]
        wt.append(w[0] * ts[0] + w[1] * ts[1] + w[2] * ts[2])
        for i in range(3):
            term = rho[s] * w[i]
            m[i] = term if s == 0 else m[i] + term
        tp = TAU[s] * psi[s]
        x.extend(tp * w[i] for i in range(3))
    m = [m[i] * inverse for i in range(3)]
    mu = m[0] * u[0] + m[1] * u[1] + m[2] * u[2]
    dens = [e_val[s] + wt[s] * (TAU[s] * (1.0 - psi[s]) - ratio[s]) - mu for s in range(3)]
    return x, m, dens


def products(y, d):
    kxx, kyy, kzz = y[0] * d[0], y[1] * d[1], y[2] * d[2]
    return [
        kxx,
        kyy,
        kzz,
        y[0] * d[1] + y[1] * d[0],
        y[0] * d[2] + y[2] * d[0],
        y[1] * d[2] + y[2] * d[1],
        kxx + kyy,
        kyy + kzz,
        kxx + kzz,
    ]


def spread(ld, dens, psi, d):
    n = [[near(ld, 3 * s + i) for i in range(3)] for s in range(3)]
    y = [divergence(*n[s]) for s in range(3)]
    diff = [{key: n[0][i][key] - n[1][i][key] for key in n[0][i]} for i in range(3)]
    z = vector_stencil(*diff)
    xx, zz, a3, kxz = near(ld, 9), near(ld, 11), near(ld, 17), near(ld, 13)
    a1, a2, kxy, kyz = near(ld, 15), near(ld, 16), near(ld, 12), near(ld, 14)
    u = 2.0 * ld(10, 0, 0) + a1["sx"] + a2["sz"]
    v = kxy["dx"] + kyz["dz"]
    quad = 2.0 * (xx["sx"] + zz["sz"]) + corner(a3) + cross(kxz) + up_y(u + v) + dn_y(u - v)
    k = 1.0 / 36.0
    back = [
        1.2 * y[1] - 0.6 * y[2] + quad,
        1.2 * y[0] - 0.6 * y[2] - quad,
        -0.6 * (y[0] + y[1]) - 0.3 * y[2] - (d[0] * z[0] + d[1] * z[1] + d[2] * z[2]),
    ]
    return [dens[s] + (k * (1.0 - psi[s])) * back[s] for s in range(3)]


KEYS = ("xx", "yy", "zz", "xy", "xz", "yz")


def late_moments(ld, extra):
    x, y, z = (near(ld, i) for i in range(3))
    axx, azz = 2.0 * x["dx"], 2.0 * z["dz"]
    ayy = 2.0 * (up_y(y["c"]) - dn_y(y["c"]))
    exz = corner_x(x) + corner_z(z)
    exy = up_y(x["dx"] + y["sx"]) + dn_y(x["dx"] - y["sx"])
    eyz = up_y(z["dz"] + y["sz"]) + dn_y(z["dz"] - y["sz"])
    a_m = (axx + ayy + azz) + (exy + exz + eyz)
    b_m = vector_stencil(x, y, z)
    c_m = dict(
        xx=axx + exy + exz,
        yy=ayy + exy + eyz,
        zz=azz + exz + eyz,
        xy=up_y(y["dx"] + x["sx"]) + dn_y(y["dx"] - x["sx"]),
        yz=up_y(y["dz"] + z["sz"]) + dn_y(y["dz"] - z["sz"]),
        xz=corner_z(x) + corner_x(z),
    )
    out = []
    for s in range(3):
        n = near(ld, 3 + s)
        g, r = gradient(n)
        c = second(n["sx"], n["sz"], corner(n), cross(n), r)
        a = 12.0 * n["c"] + 2.0 * (n["sx"] + n["sz"]) + corner(n) + c["yy"] + a_m
        b = [g[i] + b_m[i] for i in range(3)]
        c = {key: c[key] + c_m[key] for key in c}
        if s == 2:
            a = a + extra[0]
            b = [b[i] + extra[1 + i] for i in range(3)]
            c = {key: c[key] + extra[4 + i] for i, key in enumerate(KEYS)}
        out.append((a, b, c))
    return out


def along(q, m):
    out = None
    for i in range(3):
        c = VELOCITY[q][i]
        if c != 0:
            term = m[i] if c > 0 else -m[i]
            out = term if out is None else out + term
    return out

def plus(base, term):
    return base if term is None else base + term


def kernel(
    size_x,
    size_y,
    a_in,
    pe_in,
    pl_in,
    de_in,
    dl_in,
    FIN,
    A,
    NE,
    NL,
    DE,
    DL,
    F,
    FL,
    FE,
    FM,
    FG,
    PO,
    PLX,
    PRX,
    PAO,
    PER,
    PEL,
    PAL,
    PAR,
    PGO,
    PGL,
    PGR,
    PMO,
    PML,
    PMR,
    SX,
    SG,
    SL,
    SE,
    QM,
    QS,
    TB,
    EX,
    SI,
    XM,
    XS,
    LM,
    LS,
    MS,
    TS,
    W,
    lsem,
    ssem,
    rsem,
):
    gx, gy = lax.axis_index("gx"), lax.axis_index("gy")
    xu, xd = lax.rem(gx + 1, size_x), lax.rem(gx + size_x - 1, size_x)
    yr, yl = lax.rem(gy + 1, size_y), lax.rem(gy + size_y - 1, size_y)
    everyone = [(xu, gy), (xd, gy), (gx, yr), (gx, yl), (xu, yr), (xu, yl), (xd, yr), (xd, yl)]
    barrier = pltpu.get_barrier_semaphore()
    for who in everyone:
        pl.semaphore_signal(barrier, inc=1, device_id=who, device_id_type=MESH)
    loads = [
        pltpu.make_async_copy(src, dst, lsem.at[i])
        for i, (src, dst) in enumerate(
            ((pl_in, NL), (dl_in, DL), (a_in, A), (pe_in, NE), (de_in, DE))
        )
    ]
    for copy in loads:
        copy.start()

    lane = lax.broadcasted_iota(jnp.int32, (8, 128), 1)
    sub = lax.broadcasted_iota(jnp.int32, (8, 128), 0)
    c16 = lane % 16
    group16 = lane // 16
    group4 = lane // 4

    current = [0]
    sent = [0] * N_SETS

    def remote(src, dst, who):
        sent[current[0]] += math.prod(src.shape) // 128
        return pltpu.make_async_remote_copy(
            src_ref=src,
            dst_ref=dst,
            send_sem=ssem.at[0],
            recv_sem=rsem.at[current[0]],
            device_id=who,
            device_id_type=MESH,
        )

    def close():
        current[0] += 1
        return current[0] - 1

    def begin(copies):
        for copy in copies:
            copy.start()
        return close()

    def wait_rows(rows, sem):
        span = W.at[pl.ds(0, rows)]
        pltpu.make_async_copy(span, span, sem).wait()

    def arrive(number):
        wait_rows(sent[number], rsem.at[number])

    def row_copies(ref, lead, base, depth, up, down):
        out = []
        for z in range(4):
            row = base + 12 * z
            if up:
                out.append(
                    remote(
                        ref.at[lead + (pl.ds(row + 10 - depth, depth),)],
                        ref.at[lead + (pl.ds(row + 2 - depth, depth),)],
                        (xu, gy),
                    )
                )
            if down:
                out.append(
                    remote(
                        ref.at[lead + (pl.ds(row + 2, depth),)],
                        ref.at[lead + (pl.ds(row + 10, depth),)],
                        (xd, gy),
                    )
                )
        return out

    def pop_rows(ref, lead, base):
        return (
            row_copies(ref, lead + (pl.ds(0, 5),), base, 2, True, False)
            + row_copies(ref, lead + (pl.ds(14, 5),), base, 2, False, True)
            + row_copies(ref, lead + (pl.ds(5, 9),), base, 1, True, True)
        )

    def edge_copies(own, left, right, tiles, other=None):
        other = own if other is None else other
        out = []
        for who, ref, src, dst in (
            ((xu, yr), left, (6, 2), 2),
            ((xd, yr), left, (0, 2), 12),
            ((xu, yl), right, (6, 2), 2),
            ((xd, yl), right, (0, 2), 12),
            ((gx, yr), left, (0, 8), 4),
            ((gx, yl), right, (0, 8), 4),
        ):
            out.append(
                remote(
                    (own if ref is left else other).at[tiles, pl.ds(*src)],
                    ref.at[tiles, pl.ds(dst, src[1])],
                    who,
                )
            )
        return out

    def pack(acc, v, z, slot):
        moved = pltpu.roll(v, (32 * z + 4 * slot + 2) % 128, 1)
        return moved if acc is None else jnp.where(group4 == 8 * z + slot, moved, acc)

    odd = group16 % 2 == 1

    def own_strip(own, cy):
        acc = None
        for z in range(4):
            for h in range(2):
                v = own(z, h)
                base = 32 * z + 16 * h
                w = jnp.where(
                    c16 < 8,
                    pltpu.roll(v, (base - 122 - cy) % 128, 1),
                    pltpu.roll(v, (base + 10 - cy) % 128, 1),
                )
                acc = w if acc is None else jnp.where(group16 == 2 * z + h, w, acc)
        return acc

    def strip_of(own, cy, left, right, slot):
        acc = own_strip(own, cy)
        r = [pltpu.roll(right(h), (16 * h + 4 - cy - 4 * slot) % 128, 1) for h in range(2)]
        acc = jnp.where((c16 >= 6 - cy) & (c16 < 8), jnp.where(odd, r[1], r[0]), acc)
        l = [pltpu.roll(left(h), (16 * h + 8 - cy - 4 * slot) % 128, 1) for h in range(2)]
        l = jnp.where(odd, l[1], l[0])
        return jnp.where((c16 >= 8) & (c16 <= 9 - cy), l, acc)

    def store_strip(ref, f, v):
        ref[f, 1, 8:16, :] = v
        ref[f, 0, 8:16, :] = pltpu.roll(v, 32, 1)
        ref[f, 2, 8:16, :] = pltpu.roll(v, 96, 1)

    def strip_loader(ref):
        return lambda f, dx, dz: ref[f, 1 + dz, 8 + dx : 16 + dx, :]

    def flat_loader(ref, k):
        return lambda f, dx, dz: ref[f, pl.ds(8 * k + (16 + dx + 12 * dz), 8), :]

    def over_tiles(body):
        lax.fori_loop(0, 6, lambda k, carry: (body(k), carry)[1], 0, unroll=3)

    def saved(pops, dips, ref, tile0):
        acc = [None, None]
        for z in range(4):
            flow = [None] * 19
            dens = []
            for s in range(3):
                total = None
                for q in range(19):
                    f = pops[19 * s + q, z].astype(F32)
                    total = f if total is None else total + f
                    flow[q] = f if s == 0 else flow[q] + f
                dens.append(total)
            inverse = 1.0 / (dens[0] + dens[1] + dens[2])
            fields = list(dens)
            for i in range(3):
                amount = None
                for q in range(19):
                    c = VELOCITY[q][i]
                    if c != 0:
                        term = flow[q] if c > 0 else -flow[q]
                        amount = term if amount is None else amount + term
                fields.append(amount * inverse)
            fields.extend(dips[i, z].astype(F32) for i in range(3))
            for f in range(9):
                ref[f, 12 * z + 2 : 12 * z + 10, :] = fields[f]
                acc[f // 8] = pack(acc[f // 8], fields[f], z, f % 8)
        PO[tile0] = acc[0]
        PO[tile0 + 1] = acc[1]

    loads[0].wait()
    loads[1].wait()
    saved(NL, DL, FL, 0)

    loads[2].wait()

    pair = (lane % 8) // 2
    narrow = [[None] * 4, [None] * 4]
    for o, q in enumerate(ORDER):
        acc = None
        for s in range(3):
            for z in range(4):
                v = A[19 * s + q, (z + VELOCITY[q][2]) % 4]
                F[s, o, 8 + 12 * z + 2 : 8 + 12 * z + 10, :] = v
                acc = pack(acc, v, z, 2 * s)
        PAO[o, 4:12, :] = jnp.where(group4 % 2 == 1, pltpu.roll(acc, 4, 1), acc)
        for side, group in enumerate((RIGHTWARD, LEFTWARD)):
            if o in group:
                i, j = divmod(group.index(o), 4)
                moved = pltpu.roll(acc, (2 * j - 2 * side) % 128, 1)
                old = narrow[side][i]
                narrow[side][i] = moved if old is None else jnp.where(pair == j, moved, old)
    for i in range(4):
        PER[i] = narrow[0][i]
        PEL[i] = narrow[1][i]

    pl.semaphore_wait(barrier, 8)
    every = (pl.ds(0, 9),)
    lows, highs = pl.ds(0, 14), pl.ds(5, 14)
    copies = edge_copies(PER, PAL, PAR, pl.ds(0, 4), PEL)
    copies.append(remote(PAO.at[lows, pl.ds(10, 2)], PAO.at[lows, pl.ds(2, 2)], (xu, gy)))
    copies.append(remote(PAO.at[highs, pl.ds(4, 2)], PAO.at[highs, pl.ds(12, 2)], (xd, gy)))
    for copy in copies:
        copy.start()
    copies = edge_copies(PO, PLX, PRX, pl.ds(0, 2))
    copies += row_copies(FL, every, 0, 2, True, True)
    for copy in copies:
        copy.start()
    first = close()
    rows2 = begin(pop_rows(F, (pl.ds(2, 1),), 8))
    rows = begin(pop_rows(F, (pl.ds(0, 2),), 8))

    loads[3].wait()
    loads[4].wait()
    saved(NE, DE, FE, 2)
    second_set = begin(
        edge_copies(PO, PLX, PRX, pl.ds(2, 2)) + row_copies(FE, every, 0, 2, True, True)
    )

    def potentials(ref, strips):
        def body(k):
            rows = pl.ds(8 * k, 8)
            psi, fields = pick_potentials(
                [ref[s, rows, :] for s in range(3)], [ref[6 + i, rows, :] for i in range(3)]
            )
            for s in range(3):
                SI[s, k] = psi[s]
            for f in range(6):
                QM[f, pl.ds(16 + 8 * k, 8), :] = fields[f]
                QM[f, pl.ds(lax.rem(8 * k + 64, 96), 8), :] = fields[f]

        over_tiles(body)
        psi, fields = pick_potentials(
            [strips[s] for s in range(3)], [strips[6 + i] for i in range(3)]
        )
        for s in range(3):
            SI[s, 6] = psi[s]
        for f in range(6):
            store_strip(QS, f, fields[f])

    def all_thrusts(ref, strips):
        def keep(k, t, get):
            for s in range(3):
                ratio = TAU[s] * SI[s, k] / get[s]
                TB[18 + s, k] = ratio
                for i in range(3):
                    TB[3 * s + i, k] = t[3 * s + i]
                    TB[9 + 3 * s + i, k] = get[3 + i] + ratio * t[3 * s + i]
            TB[21, k] = 1.0 / (get[0] + get[1] + get[2])

        def body(k):
            rows = pl.ds(8 * k, 8)
            get = [ref[f, rows, :] for f in range(9)]
            keep(k, thrusts(flat_loader(QM, k), get[6:9]), get)

        over_tiles(body)
        get = [strips[f] for f in range(9)]
        keep(6, thrusts(strip_loader(QS), get[6:9]), get)

    def field_strips(ref, strips, tile0):
        for f in range(9):
            tile, slot = tile0 + f // 8, f % 8
            strips[f] = strip_of(
                lambda z, h: ref[f, 12 * z + 4 * h : 12 * z + 4 * h + 8, :],
                0,
                lambda h: PLX[tile, 2 + 4 * h : 10 + 4 * h, :],
                lambda h: PRX[tile, 2 + 4 * h : 10 + 4 * h, :],
                slot,
            )

    def one(mom, k, get):
        psi = [SI[s, k] for s in range(3)]
        t = [TB[f, k] for f in range(22)]
        return local_adjoint(
            mom, get[0:3], get[3:6], psi, t[0:9], t[9:18], t[18:21], t[21]
        )

    def main_stage(ref, main_moments):
        def body(k):
            rows = pl.ds(8 * k, 8)
            get = [ref[f, rows, :] for f in range(9)]
            x, m, dens = one(main_moments(k), k, get)
            for f, v in enumerate(x + products(x[6:9], get[6:9])):
                XM[f, pl.ds(16 + 8 * k, 8), :] = v
                XM[f, pl.ds(lax.rem(8 * k + 64, 96), 8), :] = v
            for f, v in enumerate(m + dens):
                LM[f, rows, :] = v

        over_tiles(body)

    def strip_stage(strips, mom):
        x, m, dens = one(mom, 6, [strips[f] for f in range(9)])
        for f in range(9):
            SX[f] = x[f]
        for f, v in enumerate(m + dens):
            LS[f, 8:16, :] = v

    def close_strips(strips, own):
        x = [SX[f] for f in range(9)]
        if own:
            inner = (c16 < 5) | (c16 >= 11)
            for f in range(9):
                v = own_strip(lambda z, h: XM[f, 16 + 12 * z + 4 * h : 24 + 12 * z + 4 * h, :], 0)
                x[f] = jnp.where(inner, v, x[f])
            for f in range(3, 6):
                v = own_strip(lambda z, h: LM[f, 12 * z + 4 * h : 8 + 12 * z + 4 * h, :], 0)
                LS[f, 8:16, :] = jnp.where(inner, v, LS[f, 8:16, :])
        for f, v in enumerate(x + products(x[6:9], [strips[6 + i] for i in range(3)])):
            store_strip(XS, f, v)

    def spread_stage(ref, strips):
        def body(k):
            rows = pl.ds(8 * k, 8)
            new = spread(
                flat_loader(XM, k),
                [LM[3 + s, rows, :] for s in range(3)],
                [SI[s, k] for s in range(3)],
                [ref[6 + i, rows, :] for i in range(3)],
            )
            for s in range(3):
                LM[3 + s, rows, :] = new[s]

        over_tiles(body)
        new = spread(
            strip_loader(XS),
            [LS[3 + s, 8:16, :] for s in range(3)],
            [SI[s, 6] for s in range(3)],
            [strips[6 + i] for i in range(3)],
        )
        for s in range(3):
            LS[3 + s, 8:16, :] = new[s]

    def folded(ref, f):
        low = ref[f, 10:18, :]
        high = pltpu.roll(ref[f, 6:14, :], 112, 1)
        return jnp.where(sub < 4, low, high)

    def with_edges(v, edge, z, width=1):
        right = pltpu.roll(edge, (122 - 32 * z) % 128, 1)
        left = pltpu.roll(edge, (-32 * z - 10) % 128, 1)
        return jnp.where(lane >= 128 - width, right, jnp.where(lane < width, left, v))

    arrive(first)
    field_strips(FL, SL, 0)
    potentials(FL, SL)
    all_thrusts(FL, SL)

    hsel, csel = group4 % 2 == 1, lane % 4 < 2
    lefts, rights = {}, {}
    for o, q in enumerate(ORDER):
        cx, cy, _ = VELOCITY[q]
        m = jnp.where(hsel, PAO[o, 6 + cx : 14 + cx, :], PAO[o, 2 + cx : 10 + cx, :])

        def received(ref, group, place):
            i, j = divmod(group.index(o), 4)
            low = pltpu.roll(ref[i, 2 + cx : 10 + cx, :], (place - 2 * j) % 128, 1)
            high = pltpu.roll(ref[i, 6 + cx : 14 + cx, :], (place + 4 - 2 * j) % 128, 1)
            return jnp.where(hsel, high, low)

        l = jnp.where(csel, received(PAL, RIGHTWARD, 0), m) if cy <= 0 else m
        r = jnp.where(csel, m, received(PAR, LEFTWARD, 2)) if cy >= 0 else m
        lefts[q] = shift_y(l, cy)
        rights[q] = shift_y(r, cy)
    lefts, rights = moments_of(lefts), moments_of(rights)

    def expanded(l, r, s):
        l = jnp.where(odd, pltpu.roll(l, (20 - 8 * s) % 128, 1), pltpu.roll(l, (8 - 8 * s) % 128, 1))
        r = jnp.where(odd, pltpu.roll(r, (16 - 8 * s) % 128, 1), pltpu.roll(r, (4 - 8 * s) % 128, 1))
        return jnp.where(c16 >= 8, l, r)

    strip_stage(
        SL,
        [
            (
                expanded(lefts[0], rights[0], s),
                [expanded(lefts[1][i], rights[1][i], s) for i in range(3)],
                {key: expanded(lefts[2][key], rights[2][key], s) for key in lefts[2]},
            )
            for s in range(3)
        ],
    )
    arrive(rows2)

    acc = [None] * 3
    for o, q in enumerate(ORDER):
        cx, cy, cz = VELOCITY[q]
        slot = o % 8
        for z in range(4):
            v = shift_y(F[2, o, 8 + 12 * z + 2 + cx : 8 + 12 * z + 10 + cx, :], cy)
            if cy == -1:
                i, j = divmod(RIGHTWARD.index(o), 4)
                halo = pltpu.roll(
                    PAL[i, 4 + cx : 12 + cx, :], (-(32 * z + 17 + 2 * j)) % 128, 1
                )
                v = jnp.where(lane == 0, halo, v)
            if cy == 1:
                i, j = divmod(LEFTWARD.index(o), 4)
                halo = pltpu.roll(
                    PAR[i, 4 + cx : 12 + cx, :], (127 - (32 * z + 16 + 2 * j)) % 128, 1
                )
                v = jnp.where(lane == 127, halo, v)
            to = (z - cz) % 4
            FG[o, 8 + 12 * to + 2 : 8 + 12 * to + 10, :] = v
            acc[o // 8] = pack(acc[o // 8], v, to, slot)
    for i in range(3):
        PGO[i] = acc[i]
    kept = begin(
        edge_copies(PGO, PGL, PGR, pl.ds(0, 3))
        + row_copies(FG, (pl.ds(0, 14),), 8, 2, True, False)
        + row_copies(FG, (pl.ds(5, 14),), 8, 2, False, True)
    )

    def pulled_moments(k):
        out = []
        for s in range(3):
            g = {}
            for o, q in enumerate(ORDER):
                cx, cy, _ = VELOCITY[q]
                g[q] = shift_y(F[s, o, pl.ds(8 * k + (8 + cx), 8), :], cy)
            out.append(moments_of(g))
        return out

    arrive(rows)
    main_stage(FL, pulled_moments)
    close_strips(SL, True)
    spread_stage(FL, SL)

    acc = None
    for f in range(6):
        edge = folded(LS, f)
        for z in range(4):
            v = with_edges(LM[f, 12 * z + 2 : 12 * z + 10, :], edge, z, 1 + f // 3)
            FM[f, 16 + 12 * z + 2 : 16 + 12 * z + 10, :] = v
            acc = pack(acc, v, z, f)
    PMO[0] = acc
    middle = begin(
        edge_copies(PMO, PML, PMR, pl.ds(0, 1))
        + row_copies(FM, (pl.ds(0, 6),), 16, 2, True, True)
    )

    arrive(second_set)
    field_strips(FE, SE, 2)
    potentials(FE, SE)
    all_thrusts(FE, SE)

    arrive(kept)
    for o, q in enumerate(ORDER):
        cx, cy, _ = VELOCITY[q]
        SG[o] = strip_of(
            lambda z, h: FG[o, 8 + 12 * z + 4 * h + cx : 8 + 12 * z + 4 * h + cx + 8, :],
            cy,
            lambda h: PGL[o // 8, 2 + 4 * h + cx : 10 + 4 * h + cx, :],
            lambda h: PGR[o // 8, 2 + 4 * h + cx : 10 + 4 * h + cx, :],
            o % 8,
        )


    def keep_moments(k, g):
        a, b, c = moments_of(g)
        for f, v in enumerate([a, *b, *(c[key] for key in KEYS)]):
            EX[f, k] = 0.2 * v

    def kept_tile(k):
        g = {}
        for o, q in enumerate(ORDER):
            cx, cy, _ = VELOCITY[q]
            g[q] = shift_y(FG[o, pl.ds(8 * k + (8 + cx), 8), :], cy)
        keep_moments(k, g)

    over_tiles(kept_tile)
    keep_moments(6, {q: SG[SLOT[q]] for q in range(19)})

    arrive(middle)
    for f in range(6):
        FM[f, 0:16, :] = FM[f, 48:64, :]
        FM[f, 64:80, :] = FM[f, 16:32, :]
        store_strip(
            MS,
            f,
            strip_of(
                lambda z, h: FM[f, 16 + 12 * z + 4 * h : 16 + 12 * z + 4 * h + 8, :],
                0,
                lambda h: PML[0, 2 + 4 * h : 10 + 4 * h, :],
                lambda h: PMR[0, 2 + 4 * h : 10 + 4 * h, :],
                f,
            ),
        )

    def middle_moments(k):
        return late_moments(flat_loader(FM, k), [EX[f, k] for f in range(10)])

    def middle_strip_moments():
        return late_moments(strip_loader(MS), [EX[f, 6] for f in range(10)])

    main_stage(FE, middle_moments)
    strip_stage(SE, middle_strip_moments())
    close_strips(SE, False)
    spread_stage(FE, SE)

    strip = strip_loader(MS)
    for o, q in enumerate(ORDER):
        cx, cy, cz = VELOCITY[q]
        if cy != 0:
            v = plus(strip(5, cx, cz), along(q, [strip(i, cx, cz) for i in range(3)]))
            TS[o, 8:16, :] = shift_y(v, cy) + 0.2 * SG[o]

    edges = [folded(LS, f) for f in range(6)]
    for z in range(4):
        for f in range(6):
            FIN[f, z] = with_edges(LM[f, 12 * z + 2 : 12 * z + 10, :], edges[f], z, 1 + f // 3)
        for o, q in enumerate(ORDER):
            cx, cy, cz = VELOCITY[q]
            row = 12 * z + 2 + cx
            mid = [FM[i, 16 + row + 12 * cz : 24 + row + 12 * cz, :] for i in (0, 1, 2, 5)]
            v = plus(mid[3], along(q, mid[0:3])) + 0.2 * FG[o, 8 + row : 16 + row, :]
            v = shift_y(v, cy)
            if cy != 0:
                v = with_edges(v, folded(TS, o), z)
            FIN[6 + q, z] = 0.2 * v

    wait_rows(sum(sent), ssem.at[0])


def expand(fin, out, OUT, sem):
    copies = []
    for s in range(3):
        for z in range(4):
            m = [fin[i, z] for i in range(3)]
            base = fin[3 + s, z]
            for q in range(19):
                v = plus(base, along(q, m))
                OUT[19 * s + q, z] = v + fin[6 + q, z] if s == 2 else v
        part = pl.ds(19 * s, 19)
        copies.append(pltpu.make_async_copy(OUT.at[part], out.at[part], sem.at[s]))
        copies[s].start()
    for copy in copies:
        copy.wait()


def block(size_x, size_y, *args):
    def vmem(*shape, dtype=F32):
        return pltpu.VMEM(shape, dtype)

    bf = jnp.bfloat16
    scratch = [
        vmem(57, 4, 8, 128),
        vmem(57, 4, 8, 128, dtype=bf),
        vmem(57, 4, 8, 128, dtype=bf),
        vmem(3, 4, 8, 128, dtype=bf),
        vmem(3, 4, 8, 128, dtype=bf),
        vmem(3, 19, 64, 128),
        vmem(9, 48, 128),
        vmem(9, 48, 128),
        vmem(6, 80, 128),
        vmem(19, 64, 128),
        vmem(4, 8, 128),
        vmem(4, 16, 128),
        vmem(4, 16, 128),
        vmem(19, 16, 128),
        vmem(4, 8, 128),
        vmem(4, 8, 128),
        vmem(4, 16, 128),
        vmem(4, 16, 128),
        vmem(3, 8, 128),
        vmem(3, 16, 128),
        vmem(3, 16, 128),
        vmem(1, 8, 128),
        vmem(1, 16, 128),
        vmem(1, 16, 128),
        vmem(9, 8, 128),
        vmem(19, 8, 128),
        vmem(9, 8, 128),
        vmem(9, 8, 128),
        vmem(6, 96, 128),
        vmem(6, 3, 24, 128),
        vmem(22, 7, 8, 128),
        vmem(10, 7, 8, 128),
        vmem(3, 7, 8, 128),
        vmem(18, 96, 128),
        vmem(18, 3, 24, 128),
        vmem(6, 48, 128),
        vmem(6, 24, 128),
        vmem(6, 3, 24, 128),
        vmem(19, 24, 128),
        vmem(3072, 128),
        pltpu.SemaphoreType.DMA((5,)),
        pltpu.SemaphoreType.DMA((1,)),
        pltpu.SemaphoreType.DMA((N_SETS,)),
    ]
    fin = pl.pallas_call(
        lambda *refs: kernel(size_x, size_y, *refs),
        out_shape=jax.ShapeDtypeStruct((25, 4, 8, 128), F32),
        in_specs=[pl.BlockSpec(memory_space=pltpu.HBM)] * 5,
        out_specs=pl.BlockSpec(memory_space=pltpu.VMEM),
        scratch_shapes=scratch,
        compiler_params=pltpu.CompilerParams(
            collective_id=0, has_side_effects=True, vmem_limit_bytes=24 << 20
        ),
        name="lattice_adjoint",
    )(*[pltpu.with_memory_space_constraint(a, pltpu.HBM) for a in args])
    return pl.pallas_call(
        expand,
        out_shape=jax.ShapeDtypeStruct((57, 4, 8, 128), F32),
        in_specs=[pl.BlockSpec(memory_space=pltpu.VMEM)],
        out_specs=pl.BlockSpec(memory_space=pltpu.HBM),
        scratch_shapes=[vmem(57, 4, 8, 128), pltpu.SemaphoreType.DMA((3,))],
        compiler_params=pltpu.CompilerParams(vmem_limit_bytes=8 << 20),
        name="lattice_expand",
    )(fin)


def solution(mesh):
    size_x, size_y = mesh.shape["gx"], mesh.shape["gy"]
    spec = P(None, None, "gx", "gy")
    return jax.shard_map(
        lambda *args: block(size_x, size_y, *args),
        mesh=mesh,
        in_specs=(spec,) * 5,
        out_specs=spec,
        check_vma=False,
    )
```

```python
import math

import jax
import jax.numpy as jnp
from jax import lax
from jax.experimental import pallas as pl
from jax.experimental.pallas import tpu as pltpu
from jax.sharding import PartitionSpec as P

MESH = pl.DeviceIdType.MESH
VELOCITY = (
    (1, 0, 0),
    (-1, 0, 0),
    (0, 1, 0),
    (0, -1, 0),
    (1, 1, 0),
    (-1, -1, 0),
    (1, -1, 0),
    (-1, 1, 0),
    (1, 0, 1),
    (-1, 0, -1),
    (1, 0, -1),
    (-1, 0, 1),
    (0, 1, 1),
    (0, -1, -1),
    (0, 1, -1),
    (0, -1, 1),
    (0, 0, 0),
    (0, 0, 1),
    (0, 0, -1),
)
TAU = (1.0, 1.0, 1.25)
G = ((0.0, 1.2, -0.6), (1.2, 0.0, -0.6), (-0.6, -0.6, -0.3))
ORDER = (1, 5, 7, 9, 11, 2, 3, 12, 13, 14, 15, 16, 17, 18, 0, 4, 6, 8, 10)
SLOT = {q: i for i, q in enumerate(ORDER)}
RIGHTWARD = tuple(o for o, q in enumerate(ORDER) if VELOCITY[q][1] <= 0)
LEFTWARD = tuple(o for o, q in enumerate(ORDER) if VELOCITY[q][1] >= 0)
F32 = jnp.float32
N_SETS = 8


def up_y(v):
    return pltpu.roll(v, 127, 1)


def dn_y(v):
    return pltpu.roll(v, 1, 1)


def shift_y(v, cy):
    return v if cy == 0 else (up_y(v) if cy == 1 else dn_y(v))


def near(ld, f):
    n = dict(
        c=ld(f, 0, 0),
        xp=ld(f, 1, 0),
        xm=ld(f, -1, 0),
        zp=ld(f, 0, 1),
        zm=ld(f, 0, -1),
        pp=ld(f, 1, 1),
        pm=ld(f, 1, -1),
        mp=ld(f, -1, 1),
        mm=ld(f, -1, -1),
    )
    n["dx"] = n["xp"] - n["xm"]
    n["dz"] = n["zp"] - n["zm"]
    n["sx"] = n["xp"] + n["xm"]
    n["sz"] = n["zp"] + n["zm"]
    return n


def corner(n):
    return (n["pp"] + n["mm"]) + (n["pm"] + n["mp"])


def cross(n):
    return (n["pp"] + n["mm"]) - (n["pm"] + n["mp"])


def corner_x(n):
    return (n["pp"] - n["mm"]) + (n["pm"] - n["mp"])


def corner_z(n):
    return (n["pp"] - n["mm"]) - (n["pm"] - n["mp"])


def gradient(n):
    h = 2.0 * n["c"] + n["sx"] + n["sz"]
    r = dict(
        hp=up_y(h),
        hm=dn_y(h),
        dxp=up_y(n["dx"]),
        dxm=dn_y(n["dx"]),
        dzp=up_y(n["dz"]),
        dzm=dn_y(n["dz"]),
    )
    gx = 2.0 * n["dx"] + corner_x(n) + (r["dxp"] + r["dxm"])
    gz = 2.0 * n["dz"] + corner_z(n) + (r["dzp"] + r["dzm"])
    return (gx, r["hp"] - r["hm"], gz), r


def second(sx, sz, cor, crs, r):
    xx = 2.0 * sx + cor + (up_y(sx) + dn_y(sx))
    zz = 2.0 * sz + cor + (up_y(sz) + dn_y(sz))
    return dict(
        xx=xx,
        yy=r["hp"] + r["hm"],
        zz=zz,
        xy=r["dxp"] - r["dxm"],
        yz=r["dzp"] - r["dzm"],
        xz=crs,
    )


def vector_stencil(nx, ny, nz):
    px = 2.0 * nx["sx"] + corner(nx) + cross(nz)
    px = px + up_y(nx["sx"] + ny["dx"]) + dn_y(nx["sx"] - ny["dx"])
    pz = 2.0 * nz["sz"] + corner(nz) + cross(nx)
    pz = pz + up_y(nz["sz"] + ny["dz"]) + dn_y(nz["sz"] - ny["dz"])
    a = 2.0 * ny["c"] + ny["sx"] + ny["sz"]
    b = nx["dx"] + nz["dz"]
    return px, up_y(a + b) + dn_y(a - b), pz


def divergence(nx, ny, nz):
    u = nx["dx"] + nz["dz"]
    v = 2.0 * ny["c"] + ny["sx"] + ny["sz"]
    return 2.0 * u + corner_x(nx) + corner_z(nz) + up_y(u + v) + dn_y(u - v)


def moments_of(g):
    p = {}
    m = {}
    for q in (0, 2, 4, 6, 8, 10, 12, 14, 17):
        p[q] = g[q] + g[q + 1]
        m[q] = g[q] - g[q + 1]
    xy, xz, yz = p[4] + p[6], p[8] + p[10], p[12] + p[14]
    ax, ay, az = 2.0 * p[0], 2.0 * p[2], 2.0 * p[17]
    a = 12.0 * g[16] + (ax + ay + az) + (xy + xz + yz)
    b = (
        2.0 * m[0] + (m[4] + m[6]) + (m[8] + m[10]),
        2.0 * m[2] + (m[4] - m[6]) + (m[12] + m[14]),
        2.0 * m[17] + (m[8] - m[10]) + (m[12] - m[14]),
    )
    c = dict(
        xx=ax + xy + xz,
        yy=ay + xy + yz,
        zz=az + xz + yz,
        xy=p[4] - p[6],
        xz=p[8] - p[10],
        yz=p[12] - p[14],
    )
    return a, b, c


def pick_potentials(rho, d):
    psi = [1.0 - jnp.exp(-r) for r in rho]
    mixed = [
        1.2 * psi[1] - 0.6 * psi[2],
        1.2 * psi[0] - 0.6 * psi[2],
        -0.6 * (psi[0] + psi[1]) - 0.3 * psi[2],
    ]
    return psi, mixed + [d[j] * psi[2] for j in range(3)]


def thrusts(ld, d):
    grads, rolled, sums = [], [], []
    for s in range(3):
        n = near(ld, s)
        g, r = gradient(n)
        grads.append(g)
        if s < 2:
            rolled.append(r)
            sums.append((n["sx"], n["sz"], corner(n), cross(n)))
    diff = [b - a for a, b in zip(*sums)]
    r = {key: rolled[1][key] - rolled[0][key] for key in rolled[0]}
    m = second(*diff, r)
    e = [near(ld, 3 + j) for j in range(3)]
    p = vector_stencil(*e)
    k = 1.0 / 36.0
    k2 = 1.0 / (36.0 * 1.2)
    turned = (
        m["xx"] * d[0] + m["xy"] * d[1] + m["xz"] * d[2],
        m["xy"] * d[0] + m["yy"] * d[1] + m["yz"] * d[2],
        m["xz"] * d[0] + m["yz"] * d[1] + m["zz"] * d[2],
    )
    t0 = [-k * (grads[0][i] + p[i]) for i in range(3)]
    t1 = [k * (p[i] - grads[1][i]) for i in range(3)]
    t2 = [k2 * turned[i] - k * grads[2][i] for i in range(3)]
    return t0 + t1 + t2


def local_adjoint(mom, rho, u, psi, t, velocity, ratio, inverse):
    x, e_val, wt = [], [], []
    m = [None] * 3
    for s in range(3):
        a, b, c = mom[s]
        ts = t[3 * s : 3 * s + 3]
        v = velocity[3 * s : 3 * s + 3]
        cv = (
            c["xx"] * v[0] + c["xy"] * v[1] + c["xz"] * v[2],
            c["xy"] * v[0] + c["yy"] * v[1] + c["yz"] * v[2],
            c["xz"] * v[0] + c["yz"] * v[1] + c["zz"] * v[2],
        )
        k = 1.0 / (36.0 * TAU[s])
        b3 = [3.0 * b[i] for i in range(3)]
        a3 = 3.0 * a
        w = [b3[i] + 9.0 * cv[i] - a3 * v[i] for i in range(3)]
        half = (b3[0] + w[0]) * v[0] + (b3[1] + w[1]) * v[1] + (b3[2] + w[2]) * v[2]
        e_val.append(k * a + (0.5 * k) * half)
        w = [k * w[i] for i in range(3)]
        wt.append(w[0] * ts[0] + w[1] * ts[1] + w[2] * ts[2])
        for i in range(3):
            term = rho[s] * w[i]
            m[i] = term if s == 0 else m[i] + term
        tp = TAU[s] * psi[s]
        x.extend(tp * w[i] for i in range(3))
    m = [m[i] * inverse for i in range(3)]
    mu = m[0] * u[0] + m[1] * u[1] + m[2] * u[2]
    dens = [e_val[s] + wt[s] * (TAU[s] * (1.0 - psi[s]) - ratio[s]) - mu for s in range(3)]
    return x, m, dens


def products(y, d):
    kxx, kyy, kzz = y[0] * d[0], y[1] * d[1], y[2] * d[2]
    return [
        kxx,
        kyy,
        kzz,
        y[0] * d[1] + y[1] * d[0],
        y[0] * d[2] + y[2] * d[0],
        y[1] * d[2] + y[2] * d[1],
        kxx + kyy,
        kyy + kzz,
        kxx + kzz,
    ]


def spread(ld, dens, psi, d):
    n = [[near(ld, 3 * s + i) for i in range(3)] for s in range(3)]
    y = [divergence(*n[s]) for s in range(3)]
    diff = [{key: n[0][i][key] - n[1][i][key] for key in n[0][i]} for i in range(3)]
    z = vector_stencil(*diff)
    xx, zz, a3, kxz = near(ld, 9), near(ld, 11), near(ld, 17), near(ld, 13)
    a1, a2, kxy, kyz = near(ld, 15), near(ld, 16), near(ld, 12), near(ld, 14)
    u = 2.0 * ld(10, 0, 0) + a1["sx"] + a2["sz"]
    v = kxy["dx"] + kyz["dz"]
    quad = 2.0 * (xx["sx"] + zz["sz"]) + corner(a3) + cross(kxz) + up_y(u + v) + dn_y(u - v)
    k = 1.0 / 36.0
    back = [
        1.2 * y[1] - 0.6 * y[2] + quad,
        1.2 * y[0] - 0.6 * y[2] - quad,
        -0.6 * (y[0] + y[1]) - 0.3 * y[2] - (d[0] * z[0] + d[1] * z[1] + d[2] * z[2]),
    ]
    return [dens[s] + (k * (1.0 - psi[s])) * back[s] for s in range(3)]


KEYS = ("xx", "yy", "zz", "xy", "xz", "yz")


def late_moments(ld, extra):
    x, y, z = (near(ld, i) for i in range(3))
    axx, azz = 2.0 * x["dx"], 2.0 * z["dz"]
    ayy = 2.0 * (up_y(y["c"]) - dn_y(y["c"]))
    exz = corner_x(x) + corner_z(z)
    exy = up_y(x["dx"] + y["sx"]) + dn_y(x["dx"] - y["sx"])
    eyz = up_y(z["dz"] + y["sz"]) + dn_y(z["dz"] - y["sz"])
    a_m = (axx + ayy + azz) + (exy + exz + eyz)
    b_m = vector_stencil(x, y, z)
    c_m = dict(
        xx=axx + exy + exz,
        yy=ayy + exy + eyz,
        zz=azz + exz + eyz,
        xy=up_y(y["dx"] + x["sx"]) + dn_y(y["dx"] - x["sx"]),
        yz=up_y(y["dz"] + z["sz"]) + dn_y(y["dz"] - z["sz"]),
        xz=corner_z(x) + corner_x(z),
    )
    out = []
    for s in range(3):
        n = near(ld, 3 + s)
        g, r = gradient(n)
        c = second(n["sx"], n["sz"], corner(n), cross(n), r)
        a = 12.0 * n["c"] + 2.0 * (n["sx"] + n["sz"]) + corner(n) + c["yy"] + a_m
        b = [g[i] + b_m[i] for i in range(3)]
        c = {key: c[key] + c_m[key] for key in c}
        if s == 2:
            a = a + extra[0]
            b = [b[i] + extra[1 + i] for i in range(3)]
            c = {key: c[key] + extra[4 + i] for i, key in enumerate(KEYS)}
        out.append((a, b, c))
    return out


def along(q, m):
    out = None
    for i in range(3):
        c = VELOCITY[q][i]
        if c != 0:
            term = m[i] if c > 0 else -m[i]
            out = term if out is None else out + term
    return out

def plus(base, term):
    return base if term is None else base + term


def kernel(
    size_x,
    size_y,
    a_in,
    pe_in,
    pl_in,
    de_in,
    dl_in,
    FIN,
    A,
    NE,
    NL,
    DE,
    DL,
    F,
    FL,
    FE,
    FM,
    FG,
    PO,
    PLX,
    PRX,
    PAO,
    PER,
    PEL,
    PAL,
    PAR,
    PGO,
    PGL,
    PGR,
    PMO,
    PML,
    PMR,
    SX,
    SG,
    SL,
    SE,
    QM,
    QS,
    TB,
    EX,
    SI,
    XM,
    XS,
    LM,
    LS,
    MS,
    TS,
    W,
    lsem,
    ssem,
    rsem,
):
    gx, gy = lax.axis_index("gx"), lax.axis_index("gy")
    xu, xd = lax.rem(gx + 1, size_x), lax.rem(gx + size_x - 1, size_x)
    yr, yl = lax.rem(gy + 1, size_y), lax.rem(gy + size_y - 1, size_y)
    everyone = [(xu, gy), (xd, gy), (gx, yr), (gx, yl), (xu, yr), (xu, yl), (xd, yr), (xd, yl)]
    barrier = pltpu.get_barrier_semaphore()
    for who in everyone:
        pl.semaphore_signal(barrier, inc=1, device_id=who, device_id_type=MESH)
    loads = [
        pltpu.make_async_copy(src, dst, lsem.at[i])
        for i, (src, dst) in enumerate(
            ((pl_in, NL), (dl_in, DL), (a_in, A), (pe_in, NE), (de_in, DE))
        )
    ]
    for copy in loads:
        copy.start()

    lane = lax.broadcasted_iota(jnp.int32, (8, 128), 1)
    sub = lax.broadcasted_iota(jnp.int32, (8, 128), 0)
    c16 = lane % 16
    group16 = lane // 16
    group4 = lane // 4

    current = [0]
    sent = [0] * N_SETS

    def remote(src, dst, who):
        sent[current[0]] += math.prod(src.shape) // 128
        return pltpu.make_async_remote_copy(
            src_ref=src,
            dst_ref=dst,
            send_sem=ssem.at[0],
            recv_sem=rsem.at[current[0]],
            device_id=who,
            device_id_type=MESH,
        )

    def close():
        current[0] += 1
        return current[0] - 1

    def begin(copies):
        for copy in copies:
            copy.start()
        return close()

    def wait_rows(rows, sem):
        span = W.at[pl.ds(0, rows)]
        pltpu.make_async_copy(span, span, sem).wait()

    def arrive(number):
        wait_rows(sent[number], rsem.at[number])

    def row_copies(ref, lead, base, depth, up, down):
        out = []
        for z in range(4):
            row = base + 12 * z
            if up:
                out.append(
                    remote(
                        ref.at[lead + (pl.ds(row + 10 - depth, depth),)],
                        ref.at[lead + (pl.ds(row + 2 - depth, depth),)],
                        (xu, gy),
                    )
                )
            if down:
                out.append(
                    remote(
                        ref.at[lead + (pl.ds(row + 2, depth),)],
                        ref.at[lead + (pl.ds(row + 10, depth),)],
                        (xd, gy),
                    )
                )
        return out

    def pop_rows(ref, lead, base):
        return (
            row_copies(ref, lead + (pl.ds(0, 5),), base, 2, True, False)
            + row_copies(ref, lead + (pl.ds(14, 5),), base, 2, False, True)
            + row_copies(ref, lead + (pl.ds(5, 9),), base, 1, True, True)
        )

    def edge_copies(own, left, right, tiles, other=None):
        other = own if other is None else other
        out = []
        for who, ref, src, dst in (
            ((xu, yr), left, (6, 2), 2),
            ((xd, yr), left, (0, 2), 12),
            ((xu, yl), right, (6, 2), 2),
            ((xd, yl), right, (0, 2), 12),
            ((gx, yr), left, (0, 8), 4),
            ((gx, yl), right, (0, 8), 4),
        ):
            out.append(
                remote(
                    (own if ref is left else other).at[tiles, pl.ds(*src)],
                    ref.at[tiles, pl.ds(dst, src[1])],
                    who,
                )
            )
        return out

    def pack(acc, v, z, slot):
        moved = pltpu.roll(v, (32 * z + 4 * slot + 2) % 128, 1)
        return moved if acc is None else jnp.where(group4 == 8 * z + slot, moved, acc)

    odd = group16 % 2 == 1

    def own_strip(own, cy):
        acc = None
        for z in range(4):
            for h in range(2):
                v = own(z, h)
                base = 32 * z + 16 * h
                w = jnp.where(
                    c16 < 8,
                    pltpu.roll(v, (base - 122 - cy) % 128, 1),
                    pltpu.roll(v, (base + 10 - cy) % 128, 1),
                )
                acc = w if acc is None else jnp.where(group16 == 2 * z + h, w, acc)
        return acc

    def strip_of(own, cy, left, right, slot):
        acc = own_strip(own, cy)
        r = [pltpu.roll(right(h), (16 * h + 4 - cy - 4 * slot) % 128, 1) for h in range(2)]
        acc = jnp.where((c16 >= 6 - cy) & (c16 < 8), jnp.where(odd, r[1], r[0]), acc)
        l = [pltpu.roll(left(h), (16 * h + 8 - cy - 4 * slot) % 128, 1) for h in range(2)]
        l = jnp.where(odd, l[1], l[0])
        return jnp.where((c16 >= 8) & (c16 <= 9 - cy), l, acc)

    def store_strip(ref, f, v):
        ref[f, 1, 8:16, :] = v
        ref[f, 0, 8:16, :] = pltpu.roll(v, 32, 1)
        ref[f, 2, 8:16, :] = pltpu.roll(v, 96, 1)

    def strip_loader(ref):
        return lambda f, dx, dz: ref[f, 1 + dz, 8 + dx : 16 + dx, :]

    def flat_loader(ref, k):
        return lambda f, dx, dz: ref[f, pl.ds(8 * k + (16 + dx + 12 * dz), 8), :]

    def over_tiles(body):
        lax.fori_loop(0, 6, lambda k, carry: (body(k), carry)[1], 0, unroll=3)

    def saved(pops, dips, ref, tile0):
        acc = [None, None]
        for z in range(4):
            flow = [None] * 19
            dens = []
            for s in range(3):
                total = None
                for q in range(19):
                    f = pops[19 * s + q, z].astype(F32)
                    total = f if total is None else total + f
                    flow[q] = f if s == 0 else flow[q] + f
                dens.append(total)
            inverse = 1.0 / (dens[0] + dens[1] + dens[2])
            fields = list(dens)
            for i in range(3):
                amount = None
                for q in range(19):
                    c = VELOCITY[q][i]
                    if c != 0:
                        term = flow[q] if c > 0 else -flow[q]
                        amount = term if amount is None else amount + term
                fields.append(amount * inverse)
            fields.extend(dips[i, z].astype(F32) for i in range(3))
            for f in range(9):
                ref[f, 12 * z + 2 : 12 * z + 10, :] = fields[f]
                acc[f // 8] = pack(acc[f // 8], fields[f], z, f % 8)
        PO[tile0] = acc[0]
        PO[tile0 + 1] = acc[1]

    loads[0].wait()
    loads[1].wait()
    saved(NL, DL, FL, 0)

    loads[2].wait()

    pair = (lane % 8) // 2
    narrow = [[None] * 4, [None] * 4]
    for o, q in enumerate(ORDER):
        acc = None
        for s in range(3):
            for z in range(4):
                v = A[19 * s + q, (z + VELOCITY[q][2]) % 4]
                F[s, o, 8 + 12 * z + 2 : 8 + 12 * z + 10, :] = v
                acc = pack(acc, v, z, 2 * s)
        PAO[o, 4:12, :] = jnp.where(group4 % 2 == 1, pltpu.roll(acc, 4, 1), acc)
        for side, group in enumerate((RIGHTWARD, LEFTWARD)):
            if o in group:
                i, j = divmod(group.index(o), 4)
                moved = pltpu.roll(acc, (2 * j - 2 * side) % 128, 1)
                old = narrow[side][i]
                narrow[side][i] = moved if old is None else jnp.where(pair == j, moved, old)
    for i in range(4):
        PER[i] = narrow[0][i]
        PEL[i] = narrow[1][i]

    pl.semaphore_wait(barrier, 8)
    every = (pl.ds(0, 9),)
    lows, highs = pl.ds(0, 14), pl.ds(5, 14)
    copies = edge_copies(PER, PAL, PAR, pl.ds(0, 4), PEL)
    copies.append(remote(PAO.at[lows, pl.ds(10, 2)], PAO.at[lows, pl.ds(2, 2)], (xu, gy)))
    copies.append(remote(PAO.at[highs, pl.ds(4, 2)], PAO.at[highs, pl.ds(12, 2)], (xd, gy)))
    for copy in copies:
        copy.start()
    first = begin(edge_copies(PO, PLX, PRX, pl.ds(0, 2)))
    state_rows = begin(row_copies(FL, every, 0, 2, True, True))
    rows2 = begin(pop_rows(F, (pl.ds(2, 1),), 8))
    rows = begin(pop_rows(F, (pl.ds(0, 2),), 8))

    loads[3].wait()
    loads[4].wait()
    saved(NE, DE, FE, 2)
    second_set = begin(
        edge_copies(PO, PLX, PRX, pl.ds(2, 2)) + row_copies(FE, every, 0, 2, True, True)
    )

    def potentials(ref):
        def body(k):
            rows = pl.ds(8 * k, 8)
            psi, fields = pick_potentials(
                [ref[s, rows, :] for s in range(3)], [ref[6 + i, rows, :] for i in range(3)]
            )
            for s in range(3):
                SI[s, k] = psi[s]
            for f in range(6):
                QM[f, pl.ds(16 + 8 * k, 8), :] = fields[f]
                QM[f, pl.ds(lax.rem(8 * k + 64, 96), 8), :] = fields[f]

        over_tiles(body)

    def strip_potentials(strips):
        psi, fields = pick_potentials(
            [strips[s] for s in range(3)], [strips[6 + i] for i in range(3)]
        )
        for s in range(3):
            SI[s, 6] = psi[s]
        for f in range(6):
            store_strip(QS, f, fields[f])

    def keep(k, t, get):
        for s in range(3):
            ratio = TAU[s] * SI[s, k] / get[s]
            TB[18 + s, k] = ratio
            for i in range(3):
                TB[3 * s + i, k] = t[3 * s + i]
                TB[9 + 3 * s + i, k] = get[3 + i] + ratio * t[3 * s + i]
        TB[21, k] = 1.0 / (get[0] + get[1] + get[2])

    def main_thrusts(ref):
        def body(k):
            rows = pl.ds(8 * k, 8)
            get = [ref[f, rows, :] for f in range(9)]
            keep(k, thrusts(flat_loader(QM, k), get[6:9]), get)

        over_tiles(body)

    def strip_thrusts(strips):
        get = [strips[f] for f in range(9)]
        keep(6, thrusts(strip_loader(QS), get[6:9]), get)

    def field_strips(ref, strips, tile0):
        for f in range(9):
            tile, slot = tile0 + f // 8, f % 8
            strips[f] = strip_of(
                lambda z, h: ref[f, 12 * z + 4 * h : 12 * z + 4 * h + 8, :],
                0,
                lambda h: PLX[tile, 2 + 4 * h : 10 + 4 * h, :],
                lambda h: PRX[tile, 2 + 4 * h : 10 + 4 * h, :],
                slot,
            )

    def one(mom, k, get):
        psi = [SI[s, k] for s in range(3)]
        t = [TB[f, k] for f in range(22)]
        return local_adjoint(
            mom, get[0:3], get[3:6], psi, t[0:9], t[9:18], t[18:21], t[21]
        )

    def main_stage(ref, main_moments):
        def body(k):
            rows = pl.ds(8 * k, 8)
            get = [ref[f, rows, :] for f in range(9)]
            x, m, dens = one(main_moments(k), k, get)
            for f, v in enumerate(x + products(x[6:9], get[6:9])):
                XM[f, pl.ds(16 + 8 * k, 8), :] = v
                XM[f, pl.ds(lax.rem(8 * k + 64, 96), 8), :] = v
            for f, v in enumerate(m + dens):
                LM[f, rows, :] = v

        over_tiles(body)

    def strip_stage(strips, mom):
        x, m, dens = one(mom, 6, [strips[f] for f in range(9)])
        for f in range(9):
            SX[f] = x[f]
        for f, v in enumerate(m + dens):
            LS[f, 8:16, :] = v

    def close_strips(strips, own):
        x = [SX[f] for f in range(9)]
        if own:
            inner = (c16 < 5) | (c16 >= 11)
            for f in range(9):
                v = own_strip(lambda z, h: XM[f, 16 + 12 * z + 4 * h : 24 + 12 * z + 4 * h, :], 0)
                x[f] = jnp.where(inner, v, x[f])
            for f in range(3, 6):
                v = own_strip(lambda z, h: LM[f, 12 * z + 4 * h : 8 + 12 * z + 4 * h, :], 0)
                LS[f, 8:16, :] = jnp.where(inner, v, LS[f, 8:16, :])
        for f, v in enumerate(x + products(x[6:9], [strips[6 + i] for i in range(3)])):
            store_strip(XS, f, v)

    def main_spread(ref):
        def body(k):
            rows = pl.ds(8 * k, 8)
            new = spread(
                flat_loader(XM, k),
                [LM[3 + s, rows, :] for s in range(3)],
                [SI[s, k] for s in range(3)],
                [ref[6 + i, rows, :] for i in range(3)],
            )
            for s in range(3):
                LM[3 + s, rows, :] = new[s]

        over_tiles(body)

    def strip_spread(strips):
        new = spread(
            strip_loader(XS),
            [LS[3 + s, 8:16, :] for s in range(3)],
            [SI[s, 6] for s in range(3)],
            [strips[6 + i] for i in range(3)],
        )
        for s in range(3):
            LS[3 + s, 8:16, :] = new[s]

    def folded(ref, f):
        low = ref[f, 10:18, :]
        high = pltpu.roll(ref[f, 6:14, :], 112, 1)
        return jnp.where(sub < 4, low, high)

    def with_edges(v, edge, z, width=1):
        right = pltpu.roll(edge, (122 - 32 * z) % 128, 1)
        left = pltpu.roll(edge, (-32 * z - 10) % 128, 1)
        return jnp.where(lane >= 128 - width, right, jnp.where(lane < width, left, v))

    arrive(state_rows)
    potentials(FL)
    main_thrusts(FL)
    arrive(first)
    field_strips(FL, SL, 0)
    strip_potentials(SL)
    strip_thrusts(SL)

    hsel, csel = group4 % 2 == 1, lane % 4 < 2
    lefts, rights = {}, {}
    for o, q in enumerate(ORDER):
        cx, cy, _ = VELOCITY[q]
        m = jnp.where(hsel, PAO[o, 6 + cx : 14 + cx, :], PAO[o, 2 + cx : 10 + cx, :])

        def received(ref, group, place):
            i, j = divmod(group.index(o), 4)
            low = pltpu.roll(ref[i, 2 + cx : 10 + cx, :], (place - 2 * j) % 128, 1)
            high = pltpu.roll(ref[i, 6 + cx : 14 + cx, :], (place + 4 - 2 * j) % 128, 1)
            return jnp.where(hsel, high, low)

        l = jnp.where(csel, received(PAL, RIGHTWARD, 0), m) if cy <= 0 else m
        r = jnp.where(csel, m, received(PAR, LEFTWARD, 2)) if cy >= 0 else m
        lefts[q] = shift_y(l, cy)
        rights[q] = shift_y(r, cy)
    lefts, rights = moments_of(lefts), moments_of(rights)

    def expanded(l, r, s):
        l = jnp.where(odd, pltpu.roll(l, (20 - 8 * s) % 128, 1), pltpu.roll(l, (8 - 8 * s) % 128, 1))
        r = jnp.where(odd, pltpu.roll(r, (16 - 8 * s) % 128, 1), pltpu.roll(r, (4 - 8 * s) % 128, 1))
        return jnp.where(c16 >= 8, l, r)

    strip_stage(
        SL,
        [
            (
                expanded(lefts[0], rights[0], s),
                [expanded(lefts[1][i], rights[1][i], s) for i in range(3)],
                {key: expanded(lefts[2][key], rights[2][key], s) for key in lefts[2]},
            )
            for s in range(3)
        ],
    )
    arrive(rows2)

    acc = [None] * 3
    for o, q in enumerate(ORDER):
        cx, cy, cz = VELOCITY[q]
        slot = o % 8
        for z in range(4):
            v = shift_y(F[2, o, 8 + 12 * z + 2 + cx : 8 + 12 * z + 10 + cx, :], cy)
            if cy == -1:
                i, j = divmod(RIGHTWARD.index(o), 4)
                halo = pltpu.roll(
                    PAL[i, 4 + cx : 12 + cx, :], (-(32 * z + 17 + 2 * j)) % 128, 1
                )
                v = jnp.where(lane == 0, halo, v)
            if cy == 1:
                i, j = divmod(LEFTWARD.index(o), 4)
                halo = pltpu.roll(
                    PAR[i, 4 + cx : 12 + cx, :], (127 - (32 * z + 16 + 2 * j)) % 128, 1
                )
                v = jnp.where(lane == 127, halo, v)
            to = (z - cz) % 4
            FG[o, 8 + 12 * to + 2 : 8 + 12 * to + 10, :] = v
            acc[o // 8] = pack(acc[o // 8], v, to, slot)
    for i in range(3):
        PGO[i] = acc[i]
    kept = begin(
        edge_copies(PGO, PGL, PGR, pl.ds(0, 3))
        + row_copies(FG, (pl.ds(0, 14),), 8, 2, True, False)
        + row_copies(FG, (pl.ds(5, 14),), 8, 2, False, True)
    )

    def pulled_moments(k):
        out = []
        for s in range(3):
            g = {}
            for o, q in enumerate(ORDER):
                cx, cy, _ = VELOCITY[q]
                g[q] = shift_y(F[s, o, pl.ds(8 * k + (8 + cx), 8), :], cy)
            out.append(moments_of(g))
        return out

    arrive(rows)
    main_stage(FL, pulled_moments)
    close_strips(SL, True)
    main_spread(FL)
    strip_spread(SL)

    acc = None
    for f in range(6):
        edge = folded(LS, f)
        for z in range(4):
            v = with_edges(LM[f, 12 * z + 2 : 12 * z + 10, :], edge, z, 1 + f // 3)
            FM[f, 16 + 12 * z + 2 : 16 + 12 * z + 10, :] = v
            acc = pack(acc, v, z, f)
    PMO[0] = acc
    middle_edges = begin(edge_copies(PMO, PML, PMR, pl.ds(0, 1)))
    middle_rows = begin(row_copies(FM, (pl.ds(0, 6),), 16, 2, True, True))

    arrive(second_set)
    potentials(FE)
    main_thrusts(FE)
    field_strips(FE, SE, 2)
    strip_potentials(SE)
    strip_thrusts(SE)

    arrive(kept)
    for o, q in enumerate(ORDER):
        cx, cy, _ = VELOCITY[q]
        SG[o] = strip_of(
            lambda z, h: FG[o, 8 + 12 * z + 4 * h + cx : 8 + 12 * z + 4 * h + cx + 8, :],
            cy,
            lambda h: PGL[o // 8, 2 + 4 * h + cx : 10 + 4 * h + cx, :],
            lambda h: PGR[o // 8, 2 + 4 * h + cx : 10 + 4 * h + cx, :],
            o % 8,
        )


    def keep_moments(k, g):
        a, b, c = moments_of(g)
        for f, v in enumerate([a, *b, *(c[key] for key in KEYS)]):
            EX[f, k] = 0.2 * v

    def kept_tile(k):
        g = {}
        for o, q in enumerate(ORDER):
            cx, cy, _ = VELOCITY[q]
            g[q] = shift_y(FG[o, pl.ds(8 * k + (8 + cx), 8), :], cy)
        keep_moments(k, g)

    over_tiles(kept_tile)
    keep_moments(6, {q: SG[SLOT[q]] for q in range(19)})

    arrive(middle_rows)
    for f in range(6):
        FM[f, 0:16, :] = FM[f, 48:64, :]
        FM[f, 64:80, :] = FM[f, 16:32, :]

    def middle_moments(k):
        return late_moments(flat_loader(FM, k), [EX[f, k] for f in range(10)])

    def middle_strip_moments():
        return late_moments(strip_loader(MS), [EX[f, 6] for f in range(10)])

    main_stage(FE, middle_moments)
    main_spread(FE)
    for z in range(4):
        for o, q in enumerate(ORDER):
            cx, cy, cz = VELOCITY[q]
            row = 12 * z + 2 + cx
            mid = [FM[i, 16 + row + 12 * cz : 24 + row + 12 * cz, :] for i in (0, 1, 2, 5)]
            v = plus(mid[3], along(q, mid[0:3])) + 0.2 * FG[o, 8 + row : 16 + row, :]
            FIN[6 + q, z] = 0.2 * shift_y(v, cy)

    arrive(middle_edges)
    for f in range(6):
        store_strip(
            MS,
            f,
            strip_of(
                lambda z, h: FM[f, 16 + 12 * z + 4 * h : 16 + 12 * z + 4 * h + 8, :],
                0,
                lambda h: PML[0, 2 + 4 * h : 10 + 4 * h, :],
                lambda h: PMR[0, 2 + 4 * h : 10 + 4 * h, :],
                f,
            ),
        )
    strip_stage(SE, middle_strip_moments())
    close_strips(SE, False)
    strip_spread(SE)

    strip = strip_loader(MS)
    for o, q in enumerate(ORDER):
        cx, cy, cz = VELOCITY[q]
        if cy != 0:
            v = plus(strip(5, cx, cz), along(q, [strip(i, cx, cz) for i in range(3)]))
            TS[o, 8:16, :] = 0.2 * (shift_y(v, cy) + 0.2 * SG[o])
            edge = folded(TS, o)
            for z in range(4):
                FIN[6 + q, z] = with_edges(FIN[6 + q, z], edge, z)
    for f in range(6):
        edge = folded(LS, f)
        for z in range(4):
            FIN[f, z] = with_edges(LM[f, 12 * z + 2 : 12 * z + 10, :], edge, z, 1 + f // 3)

    wait_rows(sum(sent), ssem.at[0])


def expand(fin, out, OUT, sem):
    copies = []
    for s in range(3):
        for z in range(4):
            m = [fin[i, z] for i in range(3)]
            base = fin[3 + s, z]
            for q in range(19):
                v = plus(base, along(q, m))
                OUT[19 * s + q, z] = v + fin[6 + q, z] if s == 2 else v
        part = pl.ds(19 * s, 19)
        copies.append(pltpu.make_async_copy(OUT.at[part], out.at[part], sem.at[s]))
        copies[s].start()
    for copy in copies:
        copy.wait()


def block(size_x, size_y, *args):
    def vmem(*shape, dtype=F32):
        return pltpu.VMEM(shape, dtype)

    bf = jnp.bfloat16
    scratch = [
        vmem(57, 4, 8, 128),
        vmem(57, 4, 8, 128, dtype=bf),
        vmem(57, 4, 8, 128, dtype=bf),
        vmem(3, 4, 8, 128, dtype=bf),
        vmem(3, 4, 8, 128, dtype=bf),
        vmem(3, 19, 64, 128),
        vmem(9, 48, 128),
        vmem(9, 48, 128),
        vmem(6, 80, 128),
        vmem(19, 64, 128),
        vmem(4, 8, 128),
        vmem(4, 16, 128),
        vmem(4, 16, 128),
        vmem(19, 16, 128),
        vmem(4, 8, 128),
        vmem(4, 8, 128),
        vmem(4, 16, 128),
        vmem(4, 16, 128),
        vmem(3, 8, 128),
        vmem(3, 16, 128),
        vmem(3, 16, 128),
        vmem(1, 8, 128),
        vmem(1, 16, 128),
        vmem(1, 16, 128),
        vmem(9, 8, 128),
        vmem(19, 8, 128),
        vmem(9, 8, 128),
        vmem(9, 8, 128),
        vmem(6, 96, 128),
        vmem(6, 3, 24, 128),
        vmem(22, 7, 8, 128),
        vmem(10, 7, 8, 128),
        vmem(3, 7, 8, 128),
        vmem(18, 96, 128),
        vmem(18, 3, 24, 128),
        vmem(6, 48, 128),
        vmem(6, 24, 128),
        vmem(6, 3, 24, 128),
        vmem(19, 24, 128),
        vmem(3072, 128),
        pltpu.SemaphoreType.DMA((5,)),
        pltpu.SemaphoreType.DMA((1,)),
        pltpu.SemaphoreType.DMA((N_SETS,)),
    ]
    fin = pl.pallas_call(
        lambda *refs: kernel(size_x, size_y, *refs),
        out_shape=jax.ShapeDtypeStruct((25, 4, 8, 128), F32),
        in_specs=[pl.BlockSpec(memory_space=pltpu.HBM)] * 5,
        out_specs=pl.BlockSpec(memory_space=pltpu.VMEM),
        scratch_shapes=scratch,
        compiler_params=pltpu.CompilerParams(
            collective_id=0, has_side_effects=True, vmem_limit_bytes=24 << 20
        ),
        name="lattice_adjoint",
    )(*[pltpu.with_memory_space_constraint(a, pltpu.HBM) for a in args])
    return pl.pallas_call(
        expand,
        out_shape=jax.ShapeDtypeStruct((57, 4, 8, 128), F32),
        in_specs=[pl.BlockSpec(memory_space=pltpu.VMEM)],
        out_specs=pl.BlockSpec(memory_space=pltpu.HBM),
        scratch_shapes=[vmem(57, 4, 8, 128), pltpu.SemaphoreType.DMA((3,))],
        compiler_params=pltpu.CompilerParams(vmem_limit_bytes=8 << 20),
        name="lattice_expand",
    )(fin)


def solution(mesh):
    size_x, size_y = mesh.shape["gx"], mesh.shape["gy"]
    spec = P(None, None, "gx", "gy")
    return jax.shard_map(
        lambda *args: block(size_x, size_y, *args),
        mesh=mesh,
        in_specs=(spec,) * 5,
        out_specs=spec,
        check_vma=False,
    )
```
